768 devices in a mesh: section: 8 (over y), shard: 96 (over z, x, core).
Axes of the slice: x: 4, y: 8, z: 12, core: 2. Of those that a mesh axis runs over, the one named last changes fastest.
Arguments:
- features: bfloat16 [2, 96, 64, 1536], P(None, 'shard'), may hold values from -6 to 6
- window_building_index: int32 [2, 96], P(None, 'shard'), may hold values from 0 to 127
- building_embeddings: bfloat16 [128, 1536], replicated, may hold values from -6 to 6
- dilation_exponent: int32 [8], P('section'), may hold values from 0 to 5
- weights: bfloat16 [8, 2, 1536, 1536], P('section', None, 'shard'), may hold values from -0.109375 to 0.109375
- cotangent: bfloat16 [2, 96, 64, 1536], P(None, 'shard'), may hold values from -0.053955078 to 0.053955078
Outputs:
- grad_weights: float32 [8, 2, 1536, 1536], P('section', None, 'shard')
The draws below stay inside these ranges and needn't reach their ends.
All inputs are finite; a program needn't handle non-finite values.
Results may differ from the reference program's by a relative error of at most 0.017.
Values may be sent and summed in bfloat16 or wider, within the bound.
No kernel may reach another device: no remote copies, remote signals or barrier semaphores. Data moves between devices by JAX's collectives and lax.ppermute only.
A program may use at most 128 MiB of HBM per device.

```python
import jax
import jax.numpy as jnp
from jax import lax

C = 1536
L = 64
M = 2
BUILDINGS = 128
DILATION_LEVELS = 6
LAYER_COUNT = 8
WINDOWS = 96
TOKENS_ALL = 12288


def touch_ends(entries, rng, least, high):
    longest = entries.shape.index(max(entries.shape))
    spots = []
    for shift in (0, 1):
        where = [jax.random.randint(jax.random.fold_in(rng, axis), (), 0, length) for axis, length in enumerate(entries.shape)]
        where[longest] = (where[longest] + shift) % entries.shape[longest]
        spots.append(tuple(where))
    return entries.at[spots[0]].set(least).at[spots[1]].set(high)


def level_of(stream_key, shape, cuts, smallest, high):
    gain = 1.0
    for position, shards_of in cuts:
        draws = jax.random.uniform(jax.random.fold_in(jax.random.fold_in(stream_key, 6), position), (shards_of,), jnp.float32, smallest / len(cuts), high / len(cuts))
        gain = gain * jnp.repeat(jnp.exp(draws), shape[position] // shards_of).reshape((-1,) + (1,) * (len(shape) - 1 - position))
    return gain


def bell_draw(key, extent, scale, bound, shards=(), dtype=jnp.bfloat16):
    result = jax.random.normal(key, extent, jnp.float32) * scale
    if len(shards) > 0:
        result = level_of(key, extent, shards, -0.22, 0.18) * result
    return jnp.clip(result, min=-bound, max=bound).astype(dtype)


def setup_inputs(seed: int = 0) -> dict:
    streams_of = jax.random.split(jax.random.key(seed), 7)
    return {
        "features": bell_draw(streams_of[0], (M, WINDOWS, L, C), 1.0, 6.0, ((1, 96),)),
        "window_building_index": touch_ends(jax.random.randint(streams_of[1], (M, WINDOWS), 0, BUILDINGS), jax.random.fold_in(streams_of[1], 1), 0, BUILDINGS - 1).astype(jnp.int32),
        "building_embeddings": bell_draw(streams_of[2], (BUILDINGS, C), 1.0, 6.0),
        "dilation_exponent": touch_ends(jax.random.randint(streams_of[3], (LAYER_COUNT,), 0, DILATION_LEVELS), jax.random.fold_in(streams_of[3], 1), 0, DILATION_LEVELS - 1).astype(jnp.int32),
        "weights": bell_draw(streams_of[4], (LAYER_COUNT, 2, C, C), (2 * C) ** -0.5, 0.109375, ((0, 8), (2, 96))),
        "cotangent": bell_draw(streams_of[5], (M, WINDOWS, L, C), (TOKENS_ALL ** -0.5), 0.053955078, ((1, 96),)),
    }


def delayed(values, time_offset):
    length = values.shape[-2]
    padded = jnp.concatenate([jnp.zeros_like(values), values], axis=-2)
    return lax.dynamic_slice_in_dim(padded, (length - time_offset).astype(jnp.int32), length, axis=values.ndim - 2)

def advanced(values, time_offset):
    length = values.shape[-2]
    padded = jnp.concatenate([values, jnp.zeros_like(values)], axis=-2)
    return lax.dynamic_slice_in_dim(padded, time_offset.astype(jnp.int32), length, axis=values.ndim - 2)

def prepare(x_in, time_offset):
    width = x_in.shape[-1]
    x_full = x_in.astype(jnp.float32)
    inverse = lax.rsqrt(lax.optimization_barrier(jnp.mean(x_full * x_full, axis=-1, keepdims=True)) + 1e-06)
    normed = x_full * inverse
    rounded = normed.astype(jnp.bfloat16)
    both = jnp.concatenate([rounded, delayed(rounded, time_offset)], axis=-1).reshape(-1, 2 * width)
    return (x_full, inverse, normed, both)

def layer_forward(x_in, w_flat, time_offset):
    x_full, inverse, normed, both = prepare(x_in, time_offset)
    pre = jnp.dot(both, w_flat, preferred_element_type=jnp.float32).reshape(x_in.shape)
    return (x_full + jax.nn.silu(pre)).astype(jnp.bfloat16)

def layer_backward(x_in, upstream, w_flat, time_offset):
    width = x_in.shape[-1]
    x_full, inverse, normed, both = prepare(x_in, time_offset)
    pre = jnp.dot(both, w_flat, preferred_element_type=jnp.float32).reshape(x_in.shape)
    grad_up = upstream.astype(jnp.float32)
    sigma = jax.nn.sigmoid(pre)
    d_pre = (grad_up * sigma * (1.0 + pre * (1.0 - sigma))).astype(jnp.bfloat16).reshape(-1, width)
    grad_w = lax.dot_general(both, d_pre, (((0,), (0,)), ((), ())), preferred_element_type=jnp.float32)
    back = lax.dot_general(d_pre, w_flat, (((1,), (1,)), ((), ())), preferred_element_type=jnp.float32)
    back = back.reshape(x_in.shape[:-1] + (2 * width,))
    d_norm = back[..., :width] + advanced(back[..., width:], time_offset)
    d_x = grad_up + inverse * (d_norm - normed * lax.optimization_barrier(jnp.mean(d_norm * normed, axis=-1, keepdims=True)))
    return (d_x.astype(jnp.bfloat16), grad_w)

def reference(features, window_building_index, building_embeddings, dilation_exponent, weights, cotangent):
    width = features.shape[-1]
    bias = building_embeddings.astype(jnp.float32)[window_building_index]
    x_now = (features.astype(jnp.float32) + bias[:, :, None, :]).astype(jnp.bfloat16)
    time_offsets = jnp.left_shift(jnp.ones_like(dilation_exponent), dilation_exponent)
    saved = []
    for layer in range(LAYER_COUNT):
        saved.append(x_now)
        x_now = layer_forward(x_now, weights[layer].reshape(2 * width, width), time_offsets[layer])
    grad_now = cotangent
    results = [None] * LAYER_COUNT
    for layer in reversed(range(LAYER_COUNT)):
        grad_now, grad_w = layer_backward(saved[layer], grad_now, weights[layer].reshape(2 * width, width), time_offsets[layer])
        results[layer] = grad_w.reshape(2, width, width)
    return jnp.stack(results)
```

```python
import jax
import jax.numpy as jnp
from jax import lax
from jax.experimental import pallas as pl
from jax.experimental.pallas import tpu as pltpu
from jax.sharding import Mesh, PartitionSpec as P

SECTIONS, DEPTH, ACROSS, CORES = 8, 12, 4, 2
PARTS = DEPTH * ACROSS * CORES
OWN = 16
BLOCK = 256
SHARD = ("z", "x", "core")
GROUP = ("x", "core")


def shifted(values, hours, limit_low):
    length = values.shape[0]
    row = lax.broadcasted_iota(jnp.int32, values.shape, 0)
    if limit_low:
        return jnp.where(row >= hours, pltpu.roll(values, hours, 0), 0.0)
    return jnp.where(row < length - hours, pltpu.roll(values, length - hours, 0), 0.0)


def norm_of(x_full):
    inverse = lax.rsqrt(jnp.mean(x_full * x_full, axis=-1, keepdims=True) + 1e-06)
    return inverse, x_full * inverse


def forward_body(meta, x_ref, w_ref, keep_x, keep_z, keep_a, x_out, xs, zs, acts, now, late):
    step = pl.program_id(0)
    del keep_x, keep_z, keep_a

    @pl.when(step == 0)
    def _():
        x_full = x_ref[...].astype(jnp.float32)
        _, normed = norm_of(x_full)
        rounded = normed.astype(jnp.bfloat16)
        now[...] = rounded
        late[...] = shifted(rounded.astype(jnp.float32), meta[1], True).astype(jnp.bfloat16)
        xs[0] = x_ref[...]
        acts[0] = rounded

    rows = now.shape[1]
    pre = jnp.dot(now[...], w_ref[:, 0].reshape(rows, BLOCK), preferred_element_type=jnp.float32)
    pre += jnp.dot(late[...], w_ref[:, 1].reshape(rows, BLOCK), preferred_element_type=jnp.float32)
    zs[0] = pre
    own = x_ref[:, pl.ds(pl.multiple_of(step * BLOCK, BLOCK), BLOCK)].astype(jnp.float32)
    x_out[...] = (own + pre * jax.nn.sigmoid(pre)).astype(jnp.bfloat16)


def layer_forward(meta, x_in, w_all, xs, zs, acts):
    length, width = x_in.shape
    any_spec = pl.BlockSpec(memory_space=pl.ANY)
    return pl.pallas_call(
        forward_body,
        out_shape=(
            jax.ShapeDtypeStruct(x_in.shape, x_in.dtype),
            jax.ShapeDtypeStruct(xs.shape, xs.dtype),
            jax.ShapeDtypeStruct(zs.shape, zs.dtype),
            jax.ShapeDtypeStruct(acts.shape, acts.dtype),
        ),
        grid_spec=pltpu.PrefetchScalarGridSpec(
            num_scalar_prefetch=1,
            grid=(width // BLOCK,),
            in_specs=[
                pl.BlockSpec((length, width), lambda j, meta: (0, 0)),
                pl.BlockSpec((PARTS, 2, OWN, BLOCK), lambda j, meta: (0, 0, 0, j)),
                any_spec,
                any_spec,
                any_spec,
            ],
            out_specs=[
                pl.BlockSpec((length, BLOCK), lambda j, meta: (0, j)),
                pl.BlockSpec((1, length, width), lambda j, meta: (meta[0], 0, 0)),
                pl.BlockSpec((1, length, BLOCK), lambda j, meta: (meta[0], 0, j)),
                pl.BlockSpec((1, length, width), lambda j, meta: (meta[0], 0, 0)),
            ],
            scratch_shapes=[
                pltpu.VMEM((length, width), jnp.bfloat16),
                pltpu.VMEM((length, width), jnp.bfloat16),
            ],
        ),
        input_output_aliases={3: 1, 4: 2, 5: 3},
        compiler_params=pltpu.CompilerParams(vmem_limit_bytes=32 * 1024 * 1024),
        name="layer_forward",
    )(meta, x_in, w_all, xs, zs, acts)


def backward_body(meta, g_ref, x_ref, z_ref, w_ref, keep_d, g_out, dzs, now, early, da):
    step = pl.program_id(0)
    last = pl.num_programs(0) - 1
    del keep_d

    @pl.when(step == 0)
    def _():
        pre = z_ref[0]
        sigma = jax.nn.sigmoid(pre)
        d_pre = g_ref[...].astype(jnp.float32) * sigma * (1.0 + pre * (1.0 - sigma))
        d_pre = d_pre.astype(jnp.bfloat16)
        now[...] = d_pre
        early[...] = shifted(d_pre.astype(jnp.float32), meta[1], False).astype(jnp.bfloat16)
        dzs[0] = d_pre

    width = now.shape[1]
    dims = (((1,), (1,)), ((), ()))
    part = lax.dot_general(now[...], w_ref[:, 0].reshape(BLOCK, width), dims, preferred_element_type=jnp.float32)
    part += lax.dot_general(early[...], w_ref[:, 1].reshape(BLOCK, width), dims, preferred_element_type=jnp.float32)
    da[:, pl.ds(pl.multiple_of(step * BLOCK, BLOCK), BLOCK)] = part

    @pl.when(step == last)
    def _():
        inverse, normed = norm_of(x_ref[0].astype(jnp.float32))
        d_norm = da[...]
        mean = jnp.mean(d_norm * normed, axis=-1, keepdims=True)
        d_x = g_ref[...].astype(jnp.float32) + inverse * (d_norm - normed * mean)
        g_out[...] = d_x.astype(jnp.bfloat16)


def layer_backward(meta, g_in, xs, zs, w_all, dzs):
    length, width = g_in.shape
    return pl.pallas_call(
        backward_body,
        out_shape=(
            jax.ShapeDtypeStruct(g_in.shape, g_in.dtype),
            jax.ShapeDtypeStruct(dzs.shape, dzs.dtype),
        ),
        grid_spec=pltpu.PrefetchScalarGridSpec(
            num_scalar_prefetch=1,
            grid=(width // BLOCK,),
            in_specs=[
                pl.BlockSpec((length, width), lambda j, meta: (0, 0)),
                pl.BlockSpec((1, length, width), lambda j, meta: (meta[0], 0, 0)),
                pl.BlockSpec((1, length, width), lambda j, meta: (meta[0], 0, 0)),
                pl.BlockSpec((BLOCK // OWN, 2, OWN, width), lambda j, meta: (j, 0, 0, 0)),
                pl.BlockSpec(memory_space=pl.ANY),
            ],
            out_specs=[
                pl.BlockSpec((length, width), lambda j, meta: (0, 0)),
                pl.BlockSpec((1, length, width), lambda j, meta: (meta[0], 0, 0)),
            ],
            scratch_shapes=[
                pltpu.VMEM((length, width), jnp.bfloat16),
                pltpu.VMEM((length, width), jnp.bfloat16),
                pltpu.VMEM((length, width), jnp.float32),
            ],
        ),
        input_output_aliases={5: 1},
        compiler_params=pltpu.CompilerParams(vmem_limit_bytes=32 * 1024 * 1024),
        name="layer_backward",
    )(meta, g_in, xs, zs, w_all, dzs)


def advanced(values, hours):
    length = values.shape[-2]
    padded = jnp.concatenate([values, jnp.zeros_like(values)], axis=-2)
    return lax.dynamic_slice_in_dim(padded, hours, length, axis=values.ndim - 2)


def shards(features, index, table, exponent, weights, cotangent):
    here = lax.axis_index("section")
    micro, _, length, width = features.shape
    hours = jnp.left_shift(jnp.int32(1), exponent[0])
    onehot = (index[:, :, None] == jnp.arange(table.shape[0], dtype=jnp.int32)).astype(jnp.bfloat16)
    bias = jnp.einsum("mwb,bc->mwc", onehot, table, preferred_element_type=jnp.float32)
    inputs = (features.astype(jnp.float32) + bias[:, :, None, :]).astype(jnp.bfloat16)[:, 0]
    upstream = cotangent[:, 0]
    w_all = lax.all_gather(weights[0], SHARD, axis=0, tiled=False)

    ticks = SECTIONS + micro - 1
    slots = (micro + 1, length, width)
    xs = jnp.zeros(slots, jnp.bfloat16)
    acts = jnp.zeros(slots, jnp.bfloat16)
    zs = jnp.zeros(slots, jnp.float32)
    dzs = jnp.zeros(slots, jnp.bfloat16)

    def meta_of(order):
        inside = jnp.logical_and(order >= 0, order < micro)
        return jnp.stack([jnp.where(inside, order, micro), hours]).astype(jnp.int32)

    upward = [(i, i + 1) for i in range(SECTIONS - 1)]
    downward = [(i + 1, i) for i in range(SECTIONS - 1)]

    block = inputs[0]
    for tick in range(ticks):
        if 0 < tick < micro:
            block = jnp.where(here == 0, inputs[tick], block)
        block, xs, zs, acts = layer_forward(meta_of(tick - here), block, w_all, xs, zs, acts)
        if tick < ticks - 1:
            block = lax.ppermute(block, "section", upward)

    every = lax.all_gather(acts[:micro], GROUP, axis=0, tiled=False)

    grad = upstream[0]
    for tick in range(ticks):
        if 0 < tick < micro:
            grad = jnp.where(here == SECTIONS - 1, upstream[tick], grad)
        grad, dzs = layer_backward(meta_of(tick - (SECTIONS - 1 - here)), grad, xs, zs, w_all, dzs)
        if tick < ticks - 1:
            grad = lax.ppermute(grad, "section", downward)

    members = ACROSS * CORES
    piece = width // members
    rows = micro * length
    mine = dzs[:micro].reshape(rows, members, piece).transpose(1, 0, 2)
    theirs = lax.all_to_all(mine, GROUP, 0, 0, tiled=True)
    theirs = theirs.reshape(members * micro, length, piece)
    sides = jnp.concatenate([theirs, advanced(theirs, hours)], axis=-1).reshape(members * rows, 2 * piece)
    partial = lax.dot_general(
        every.reshape(members * rows, width), sides, (((0,), (0,)), ((), ())), preferred_element_type=jnp.float32
    ).astype(jnp.bfloat16)
    spread = lax.all_to_all(partial.reshape(DEPTH, members * OWN, 2 * piece), "z", 0, 0, tiled=True)
    total = jnp.sum(spread.astype(jnp.float32), axis=0)
    back = lax.all_to_all(total.reshape(members, OWN, 2 * piece), GROUP, 0, 0, tiled=True)
    owned = back.reshape(members, OWN, 2, piece).transpose(2, 1, 0, 3).reshape(2, OWN, width)
    return owned[None]


def solution(mesh):
    fine = Mesh(mesh.devices.reshape(SECTIONS, DEPTH, ACROSS, CORES), ("section", "z", "x", "core"))
    placed = (
        P(None, SHARD, None, None),
        P(None, SHARD),
        P(),
        P("section"),
        P("section", None, SHARD, None),
        P(None, SHARD, None, None),
    )
    return jax.shard_map(
        shards, mesh=fine, in_specs=placed, out_specs=P("section", None, SHARD, None), check_vma=False
    )
```

```python
import jax
import jax.numpy as jnp
from jax import lax
from jax.experimental import pallas as pl
from jax.experimental.pallas import tpu as pltpu
from jax.sharding import Mesh, PartitionSpec as P

SECTIONS, HIGH, LOW, ACROSS, CORES = 8, 4, 3, 4, 2
OWN = 16
BLOCK = 256
LIMIT = 20 * 1024 * 1024
SHARD = ("zh", "zl", "x", "core")
DEEP = ("zh", "zl")
ROW = ("x", "core")
WIDE = ("zl", "x", "core")


def shifted(values, hours, limit_low):
    length = values.shape[0]
    row = lax.broadcasted_iota(jnp.int32, values.shape, 0)
    if limit_low:
        return jnp.where(row >= hours, pltpu.roll(values, hours, 0), 0.0)
    return jnp.where(row < length - hours, pltpu.roll(values, length - hours, 0), 0.0)


def norm_of(x_full):
    inverse = lax.rsqrt(jnp.mean(x_full * x_full, axis=-1, keepdims=True) + 1e-06)
    return inverse, x_full * inverse


def settle_body(own_in, other_in, after, own, other, sems):
    del after
    copies = [
        pltpu.make_async_copy(own_in, own, sems.at[0]),
        pltpu.make_async_copy(other_in, other, sems.at[1]),
    ]
    for copy in copies:
        copy.start()
    for copy in copies:
        copy.wait()


def settle(own, other, after):
    size = own.size * own.dtype.itemsize
    return pl.pallas_call(
        settle_body,
        out_shape=(pltpu.VMEM(own.shape, own.dtype), pltpu.VMEM(other.shape, other.dtype)),
        in_specs=[pl.BlockSpec(memory_space=pltpu.HBM)] * 2 + [pl.BlockSpec(memory_space=pl.ANY)],
        out_specs=[pl.BlockSpec(memory_space=pltpu.VMEM)] * 2,
        scratch_shapes=[pltpu.SemaphoreType.DMA((2,))],
        cost_estimate=pl.CostEstimate(flops=0, transcendentals=0, bytes_accessed=4 * size),
        compiler_params=pltpu.CompilerParams(vmem_limit_bytes=LIMIT),
        name="settle",
    )(pltpu.with_memory_space_constraint(own, pltpu.HBM), pltpu.with_memory_space_constraint(other, pltpu.HBM), after)


def ordered(meta, current, moved):
    even = meta[2] == 0
    first = jnp.where(even, current, moved).astype(jnp.bfloat16)
    second = jnp.where(even, moved, current).astype(jnp.bfloat16)
    return first, second


def forward_body(meta, x_ref, own_ref, other_ref, keep_x, keep_z, keep_a, x_out, xs, zs, acts):
    del keep_x, keep_z, keep_a
    slot = meta[0]
    x_full = x_ref[...].astype(jnp.float32)
    _, normed = norm_of(x_full)
    rounded = normed.astype(jnp.bfloat16)
    xs[slot] = x_ref[...]
    acts[slot] = rounded
    current = rounded.astype(jnp.float32)
    first, second = ordered(meta, current, shifted(current, meta[1], True))
    for start in range(0, x_ref.shape[1], BLOCK):
        cols = slice(start, start + BLOCK)
        pre = jnp.dot(first, own_ref[:, cols], preferred_element_type=jnp.float32)
        pre += jnp.dot(second, other_ref[:, cols], preferred_element_type=jnp.float32)
        zs[slot, :, cols] = pre
        x_out[:, cols] = (x_ref[:, cols].astype(jnp.float32) + pre * jax.nn.sigmoid(pre)).astype(jnp.bfloat16)


VMEM = pl.BlockSpec(memory_space=pltpu.VMEM)
SMEM = pl.BlockSpec(memory_space=pltpu.SMEM)


def layer_forward(meta, x_in, own, other, xs, zs, acts):
    return pl.pallas_call(
        forward_body,
        out_shape=tuple(jax.ShapeDtypeStruct(v.shape, v.dtype) for v in (x_in, xs, zs, acts)),
        in_specs=[SMEM] + [VMEM] * 6,
        out_specs=[VMEM] * 4,
        input_output_aliases={4: 1, 5: 2, 6: 3},
        compiler_params=pltpu.CompilerParams(vmem_limit_bytes=LIMIT),
        name="layer_forward",
    )(meta, x_in, own, other, xs, zs, acts)


def backward_body(meta, g_ref, xs, zs, own_ref, other_ref, keep_d, g_out, dzs, da):
    del keep_d
    slot = meta[0]
    pre = zs[slot]
    sigma = jax.nn.sigmoid(pre)
    d_pre = g_ref[...].astype(jnp.float32) * sigma * (1.0 + pre * (1.0 - sigma))
    d_pre = d_pre.astype(jnp.bfloat16)
    dzs[slot] = d_pre
    current = d_pre.astype(jnp.float32)
    first, second = ordered(meta, current, shifted(current, meta[1], False))
    dims = (((1,), (1,)), ((), ()))
    for start in range(0, g_ref.shape[1], BLOCK):
        rows = slice(start, start + BLOCK)
        part = lax.dot_general(first, own_ref[rows, :], dims, preferred_element_type=jnp.float32)
        part += lax.dot_general(second, other_ref[rows, :], dims, preferred_element_type=jnp.float32)
        da[:, rows] = part
    inverse, normed = norm_of(xs[slot].astype(jnp.float32))
    d_norm = da[...]
    mean = jnp.mean(d_norm * normed, axis=-1, keepdims=True)
    g_out[...] = (g_ref[...].astype(jnp.float32) + inverse * (d_norm - normed * mean)).astype(jnp.bfloat16)


def layer_backward(meta, g_in, xs, zs, own, other, dzs):
    return pl.pallas_call(
        backward_body,
        out_shape=tuple(jax.ShapeDtypeStruct(v.shape, v.dtype) for v in (g_in, dzs)),
        in_specs=[SMEM] + [VMEM] * 6,
        out_specs=[VMEM] * 2,
        scratch_shapes=[pltpu.VMEM(g_in.shape, jnp.float32)],
        input_output_aliases={6: 1},
        compiler_params=pltpu.CompilerParams(vmem_limit_bytes=LIMIT),
        name="layer_backward",
    )(meta, g_in, xs, zs, own, other, dzs)


def advanced(values, hours):
    length = values.shape[-2]
    padded = jnp.concatenate([values, jnp.zeros_like(values)], axis=-2)
    return lax.dynamic_slice_in_dim(padded, hours, length, axis=values.ndim - 2)


def shards(features, index, table, exponent, weights, cotangent):
    here = lax.axis_index("section")
    micro, _, length, width = features.shape
    hours = jnp.left_shift(jnp.int32(1), exponent[0])
    onehot = (index[:, :, None] == jnp.arange(table.shape[0], dtype=jnp.int32)).astype(jnp.bfloat16)
    bias = jnp.einsum("mwb,bc->mwc", onehot, table, preferred_element_type=jnp.float32)
    inputs = (features.astype(jnp.float32) + bias[:, :, None, :]).astype(jnp.bfloat16)[:, 0]
    upstream = cotangent[:, 0]
    core = lax.axis_index("core")
    tap = weights[0]
    copies = jnp.broadcast_to(tap[None], (ACROSS,) + tap.shape).reshape(ACROSS * CORES * OWN, width)
    row = lax.all_to_all(copies, ROW, 0, 0, tiled=True)
    own = lax.all_gather(row, DEEP, axis=0, tiled=True)
    other = lax.ppermute(own, "core", [(0, 1), (1, 0)])
    near = settle(own, other, inputs)

    ticks = SECTIONS + micro - 1
    slots = (micro + 1, length, width)
    xs = jnp.zeros(slots, jnp.bfloat16)
    acts = jnp.zeros(slots, jnp.bfloat16)
    zs = jnp.zeros(slots, jnp.float32)
    dzs = jnp.zeros(slots, jnp.bfloat16)

    def meta_of(order):
        inside = jnp.logical_and(order >= 0, order < micro)
        return jnp.stack([jnp.where(inside, order, micro), hours, core]).astype(jnp.int32)

    upward = [(i, i + 1) for i in range(SECTIONS - 1)]
    downward = [(i + 1, i) for i in range(SECTIONS - 1)]

    block = inputs[0]
    for tick in range(ticks):
        if 0 < tick < micro:
            block = jnp.where(here == 0, inputs[tick], block)
        block, xs, zs, acts = layer_forward(meta_of(tick - here), block, *near, xs, zs, acts)
        if tick < ticks - 1:
            near = settle(own, other, block)
            block = lax.ppermute(block, "section", upward)

    every = lax.all_gather(acts[:micro], WIDE, axis=0, tiled=False)

    near = settle(own, other, upstream)
    grad = upstream[0]
    for tick in range(ticks):
        if 0 < tick < micro:
            grad = jnp.where(here == SECTIONS - 1, upstream[tick], grad)
        grad, dzs = layer_backward(meta_of(tick - (SECTIONS - 1 - here)), grad, xs, zs, *near, dzs)
        if tick < ticks - 1:
            near = settle(own, other, grad)
            grad = lax.ppermute(grad, "section", downward)

    members = LOW * ACROSS * CORES
    piece = width // members
    rows = micro * length
    mine = dzs[:micro].reshape(rows, members, piece).transpose(1, 0, 2)
    theirs = lax.all_to_all(mine, WIDE, 0, 0, tiled=True)
    theirs = theirs.reshape(members * micro, length, piece)
    sides = jnp.concatenate([theirs, advanced(theirs, hours)], axis=-1).reshape(members * rows, 2 * piece)
    partial = lax.dot_general(
        every.reshape(members * rows, width), sides, (((0,), (0,)), ((), ())), preferred_element_type=jnp.float32
    ).astype(jnp.bfloat16)
    spread = lax.all_to_all(partial.reshape(HIGH, members * OWN, 2 * piece), "zh", 0, 0, tiled=True)
    total = jnp.sum(spread.astype(jnp.float32), axis=0)
    back = lax.all_to_all(total.reshape(members, OWN, 2 * piece), WIDE, 0, 0, tiled=True)
    owned = back.reshape(members, OWN, 2, piece).transpose(2, 1, 0, 3).reshape(2, OWN, width)
    return owned[None]


def solution(mesh):
    fine = Mesh(mesh.devices.reshape(SECTIONS, HIGH, LOW, ACROSS, CORES), ("section",) + SHARD)
    placed = (
        P(None, SHARD, None, None),
        P(None, SHARD),
        P(),
        P("section"),
        P("section", None, SHARD, None),
        P(None, SHARD, None, None),
    )
    return jax.shard_map(
        shards, mesh=fine, in_specs=placed, out_specs=P("section", None, SHARD, None), check_vma=False
    )
```

```python
import jax
import jax.numpy as jnp
from jax import lax
from jax.experimental import pallas as pl
from jax.experimental.pallas import tpu as pltpu
from jax.sharding import Mesh, PartitionSpec as P

SECTIONS, HIGH, LOW, ACROSS, CORES = 8, 4, 3, 4, 2
OWN = 16
BLOCK = 256
LIMIT = 20 * 1024 * 1024
SHARD = ("zh", "zl", "x", "core")
DEEP = ("zh", "zl")
ROW = ("x", "core")
WIDE = ("zl", "x", "core")


def shifted(values, hours, limit_low):
    length = values.shape[0]
    row = lax.broadcasted_iota(jnp.int32, values.shape, 0)
    if limit_low:
        return jnp.where(row >= hours, pltpu.roll(values, hours, 0), 0.0)
    return jnp.where(row < length - hours, pltpu.roll(values, length - hours, 0), 0.0)


def norm_of(x_full):
    inverse = lax.rsqrt(jnp.mean(x_full * x_full, axis=-1, keepdims=True) + 1e-06)
    return inverse, x_full * inverse


def settle_body(*refs):
    count = (len(refs) - 2) // 2
    sems = refs[-1]
    copies = [
        pltpu.make_async_copy(refs[i], refs[count + 1 + i], sems.at[i]) for i in range(count)
    ]
    for copy in copies:
        copy.start()
    for copy in copies:
        copy.wait()


def settle(arrays, after):
    size = sum(v.size * v.dtype.itemsize for v in arrays)
    return pl.pallas_call(
        settle_body,
        out_shape=tuple(pltpu.VMEM(v.shape, v.dtype) for v in arrays),
        in_specs=[pl.BlockSpec(memory_space=pltpu.HBM)] * len(arrays) + [pl.BlockSpec(memory_space=pl.ANY)],
        out_specs=tuple(VMEM for _ in arrays),
        scratch_shapes=[pltpu.SemaphoreType.DMA((len(arrays),))],
        cost_estimate=pl.CostEstimate(flops=0, transcendentals=0, bytes_accessed=4 * size),
        compiler_params=pltpu.CompilerParams(vmem_limit_bytes=LIMIT),
        name="settle",
    )(*(pltpu.with_memory_space_constraint(v, pltpu.HBM) for v in arrays), after)


def ordered(meta, current, moved):
    even = meta[2] == 0
    first = jnp.where(even, current, moved).astype(jnp.bfloat16)
    second = jnp.where(even, moved, current).astype(jnp.bfloat16)
    return first, second


def forward_part(meta, x_ref, own_ref, other_ref, x_out, xs, zs, acts):
    slot = meta[0]
    x_full = x_ref[...].astype(jnp.float32)
    _, normed = norm_of(x_full)
    rounded = normed.astype(jnp.bfloat16)
    xs[slot] = x_ref[...]
    acts[slot] = rounded
    current = rounded.astype(jnp.float32)
    first, second = ordered(meta, current, shifted(current, meta[1], True))
    for start in range(0, x_ref.shape[1], BLOCK):
        cols = slice(start, start + BLOCK)
        pre = jnp.dot(first, own_ref[:, cols], preferred_element_type=jnp.float32)
        pre += jnp.dot(second, other_ref[:, cols], preferred_element_type=jnp.float32)
        zs[slot, :, cols] = pre
        x_out[:, cols] = (x_ref[:, cols].astype(jnp.float32) + pre * jax.nn.sigmoid(pre)).astype(jnp.bfloat16)


def backward_part(meta, g_ref, own_ref, other_ref, xs, zs, g_out, dzs, da):
    slot = meta[3]
    pre = zs[slot]
    sigma = jax.nn.sigmoid(pre)
    d_pre = g_ref[...].astype(jnp.float32) * sigma * (1.0 + pre * (1.0 - sigma))
    d_pre = d_pre.astype(jnp.bfloat16)
    dzs[slot] = d_pre
    current = d_pre.astype(jnp.float32)
    first, second = ordered(meta, current, shifted(current, meta[1], False))
    dims = (((1,), (1,)), ((), ()))
    for start in range(0, g_ref.shape[1], BLOCK):
        rows = slice(start, start + BLOCK)
        part = lax.dot_general(first, own_ref[rows, :], dims, preferred_element_type=jnp.float32)
        part += lax.dot_general(second, other_ref[rows, :], dims, preferred_element_type=jnp.float32)
        da[:, rows] = part
    inverse, normed = norm_of(xs[slot].astype(jnp.float32))
    d_norm = da[...]
    mean = jnp.mean(d_norm * normed, axis=-1, keepdims=True)
    g_out[...] = (g_ref[...].astype(jnp.float32) + inverse * (d_norm - normed * mean)).astype(jnp.bfloat16)


def forward_body(meta, x_ref, own_ref, other_ref, keep_x, keep_z, keep_a, x_out, xs, zs, acts):
    del keep_x, keep_z, keep_a
    forward_part(meta, x_ref, own_ref, other_ref, x_out, xs, zs, acts)


def backward_body(meta, g_ref, own_ref, other_ref, xs, zs, keep_d, g_out, dzs, da):
    del keep_d
    backward_part(meta, g_ref, own_ref, other_ref, xs, zs, g_out, dzs, da)


def turn_body(
    meta, x_ref, g_ref, own_ref, other_ref, keep_x, keep_z, keep_a, keep_d, x_out, g_out, xs, zs, acts, dzs, da
):
    del keep_x, keep_z, keep_a, keep_d
    forward_part(meta, x_ref, own_ref, other_ref, x_out, xs, zs, acts)
    backward_part(meta, g_ref, own_ref, other_ref, xs, zs, g_out, dzs, da)


VMEM = pl.BlockSpec(memory_space=pltpu.VMEM)
SMEM = pl.BlockSpec(memory_space=pltpu.SMEM)


def run(body, name, meta, free, weights, kept, read, scratch):
    operands = (meta, *free, *weights, *read, *kept)
    first = len(operands) - len(kept)
    return pl.pallas_call(
        body,
        out_shape=tuple(jax.ShapeDtypeStruct(v.shape, v.dtype) for v in free)
        + tuple(pltpu.VMEM(v.shape, v.dtype) for v in kept),
        in_specs=[SMEM] + [VMEM] * (len(operands) - 1),
        out_specs=tuple(VMEM for _ in range(len(free) + len(kept))),
        scratch_shapes=scratch,
        input_output_aliases={first + i: len(free) + i for i in range(len(kept))},
        compiler_params=pltpu.CompilerParams(vmem_limit_bytes=LIMIT),
        name=name,
    )(*operands)


def advanced(values, hours):
    length = values.shape[-2]
    padded = jnp.concatenate([values, jnp.zeros_like(values)], axis=-2)
    return lax.dynamic_slice_in_dim(padded, hours, length, axis=values.ndim - 2)


def shards(features, index, table, exponent, weights, cotangent):
    here = lax.axis_index("section")
    micro, _, length, width = features.shape
    hours = jnp.left_shift(jnp.int32(1), exponent[0])
    onehot = (index[:, :, None] == jnp.arange(table.shape[0], dtype=jnp.int32)).astype(jnp.bfloat16)
    bias = jnp.einsum("mwb,bc->mwc", onehot, table, preferred_element_type=jnp.float32)
    inputs = (features.astype(jnp.float32) + bias[:, :, None, :]).astype(jnp.bfloat16)[:, 0]
    upstream = cotangent[:, 0]
    core = lax.axis_index("core")
    tap = weights[0]
    copies = jnp.broadcast_to(tap[None], (ACROSS,) + tap.shape).reshape(ACROSS * CORES * OWN, width)
    row = lax.all_to_all(copies, ROW, 0, 0, tiled=True)
    own = lax.all_gather(row, DEEP, axis=0, tiled=True)
    other = lax.ppermute(own, "core", [(0, 1), (1, 0)])

    ticks = SECTIONS + micro - 1
    slots = (micro + 1, length, width)
    xs = jnp.zeros(slots, jnp.bfloat16)
    acts = jnp.zeros(slots, jnp.bfloat16)
    zs = jnp.zeros(slots, jnp.float32)
    dzs = jnp.zeros(slots, jnp.bfloat16)
    scratch = [pltpu.VMEM((length, width), jnp.float32)]

    def slot_of(order):
        return jnp.where(jnp.logical_and(order >= 0, order < micro), order, micro)

    def meta_of(ahead, behind):
        parts = [slot_of(ahead - here), hours, core, slot_of(behind - (SECTIONS - 1 - here))]
        return jnp.stack(parts).astype(jnp.int32)

    upward = [(i, i + 1) for i in range(SECTIONS - 1)]
    downward = [(i + 1, i) for i in range(SECTIONS - 1)]

    block = inputs[0]
    grad = upstream[0]
    near = settle((own,), inputs) + settle((other,), inputs)
    for tick in range(ticks + SECTIONS - 1):
        behind = tick - (SECTIONS - 1)
        meta = meta_of(tick, behind)
        if 0 < tick < micro:
            block = jnp.where(here == 0, inputs[tick], block)
        if 0 < behind < micro:
            grad = jnp.where(here == SECTIONS - 1, upstream[behind], grad)
        if behind < 0:
            block, xs, zs, acts = run(forward_body, "layer_forward", meta, (block,), near, (xs, zs, acts), (), [])
            lead = block
        elif tick < ticks:
            block, grad, xs, zs, acts, dzs = run(
                turn_body, "layer_turn", meta, (block, grad), near, (xs, zs, acts, dzs), (), scratch
            )
            lead = grad
        else:
            grad, dzs = run(backward_body, "layer_backward", meta, (grad,), near, (dzs,), (xs, zs), scratch)
            lead = grad
        if tick == ticks + 1:
            every, lead = lax.optimization_barrier((every, lead))
            every = lax.all_gather(every, ROW, axis=0, tiled=False)
        if tick < ticks + SECTIONS - 2:
            near = settle((own, other), lead)
        if tick < ticks - 1:
            block = lax.ppermute(block, "section", upward)
        if 0 <= behind and tick < ticks + SECTIONS - 2:
            grad = lax.ppermute(grad, "section", downward)
        if tick == ticks - 1:
            every = lax.all_gather(acts[:micro], "zl", axis=0, tiled=False)

    members = LOW * ACROSS * CORES
    piece = width // members
    rows = micro * length
    mine = dzs[:micro].reshape(rows, members, piece).transpose(1, 0, 2)
    theirs = lax.all_to_all(mine, ROW + ("zl",), 0, 0, tiled=True)
    theirs = theirs.reshape(members * micro, length, piece)
    sides = jnp.concatenate([theirs, advanced(theirs, hours)], axis=-1).reshape(members * rows, 2 * piece)
    partial = lax.dot_general(
        every.reshape(members * rows, width), sides, (((0,), (0,)), ((), ())), preferred_element_type=jnp.float32
    ).astype(jnp.bfloat16)
    spread = lax.all_to_all(partial.reshape(HIGH, members * OWN, 2 * piece), "zh", 0, 0, tiled=True)
    total = jnp.sum(spread.astype(jnp.float32), axis=0)
    back = lax.all_to_all(total.reshape(members, OWN, 2 * piece), WIDE, 0, 0, tiled=True)
    back = back.reshape(LOW, ACROSS * CORES, OWN, 2, piece)
    owned = back.transpose(3, 2, 1, 0, 4).reshape(2, OWN, width)
    return owned[None]


def solution(mesh):
    fine = Mesh(mesh.devices.reshape(SECTIONS, HIGH, LOW, ACROSS, CORES), ("section",) + SHARD)
    placed = (
        P(None, SHARD, None, None),
        P(None, SHARD),
        P(),
        P("section"),
        P("section", None, SHARD, None),
        P(None, SHARD, None, None),
    )
    return jax.shard_map(
        shards, mesh=fine, in_specs=placed, out_specs=P("section", None, SHARD, None), check_vma=False
    )
```

```python
import jax
import jax.numpy as jnp
from jax import lax
from jax.experimental import pallas as pl
from jax.experimental.pallas import tpu as pltpu
from jax.sharding import Mesh, PartitionSpec as P

SECTIONS, HIGH, LOW, ACROSS, CORES = 8, 4, 3, 4, 2
OWN = 16
BLOCK = 256
LIMIT = 20 * 1024 * 1024
SHARD = ("zh", "zl", "x", "core")
DEEP = ("zh", "zl")
ROW = ("x", "core")
WIDE = ("zl", "x", "core")


def shifted(values, hours, limit_low):
    length = values.shape[0]
    row = lax.broadcasted_iota(jnp.int32, values.shape, 0)
    if limit_low:
        return jnp.where(row >= hours, pltpu.roll(values, hours, 0), 0.0)
    return jnp.where(row < length - hours, pltpu.roll(values, length - hours, 0), 0.0)


def norm_of(x_full):
    inverse = lax.rsqrt(jnp.mean(x_full * x_full, axis=-1, keepdims=True) + 1e-06)
    return inverse, x_full * inverse


def settle_body(*refs):
    count = (len(refs) - 2) // 2
    sems = refs[-1]
    copies = [
        pltpu.make_async_copy(refs[i], refs[count + 1 + i], sems.at[i]) for i in range(count)
    ]
    for copy in copies:
        copy.start()
    for copy in copies:
        copy.wait()


def settle(arrays, after):
    size = sum(v.size * v.dtype.itemsize for v in arrays)
    return pl.pallas_call(
        settle_body,
        out_shape=tuple(pltpu.VMEM(v.shape, v.dtype) for v in arrays),
        in_specs=[pl.BlockSpec(memory_space=pltpu.HBM)] * len(arrays) + [pl.BlockSpec(memory_space=pl.ANY)],
        out_specs=tuple(VMEM for _ in arrays),
        scratch_shapes=[pltpu.SemaphoreType.DMA((len(arrays),))],
        cost_estimate=pl.CostEstimate(flops=0, transcendentals=0, bytes_accessed=4 * size),
        compiler_params=pltpu.CompilerParams(vmem_limit_bytes=LIMIT),
        name="settle",
    )(*(pltpu.with_memory_space_constraint(v, pltpu.HBM) for v in arrays), after)


def ordered(meta, current, moved):
    even = meta[2] == 0
    first = jnp.where(even, current, moved).astype(jnp.bfloat16)
    second = jnp.where(even, moved, current).astype(jnp.bfloat16)
    return first, second


def forward_part(meta, x_ref, own_ref, other_ref, x_out, xs, zs, acts):
    slot = meta[0]
    x_full = x_ref[...].astype(jnp.float32)
    _, normed = norm_of(x_full)
    rounded = normed.astype(jnp.bfloat16)
    xs[slot] = x_ref[...]
    acts[slot] = rounded
    current = rounded.astype(jnp.float32)
    first, second = ordered(meta, current, shifted(current, meta[1], True))
    for start in range(0, x_ref.shape[1], BLOCK):
        cols = slice(start, start + BLOCK)
        pre = jnp.dot(first, own_ref[:, cols], preferred_element_type=jnp.float32)
        pre += jnp.dot(second, other_ref[:, cols], preferred_element_type=jnp.float32)
        zs[slot, :, cols] = pre
        x_out[:, cols] = (x_ref[:, cols].astype(jnp.float32) + pre * jax.nn.sigmoid(pre)).astype(jnp.bfloat16)


def backward_part(meta, g_ref, own_ref, other_ref, xs, zs, g_out, dzs, da):
    slot = meta[3]
    pre = zs[slot]
    sigma = jax.nn.sigmoid(pre)
    d_pre = g_ref[...].astype(jnp.float32) * sigma * (1.0 + pre * (1.0 - sigma))
    d_pre = d_pre.astype(jnp.bfloat16)
    dzs[slot] = d_pre
    current = d_pre.astype(jnp.float32)
    first, second = ordered(meta, current, shifted(current, meta[1], False))
    dims = (((1,), (1,)), ((), ()))
    for start in range(0, g_ref.shape[1], BLOCK):
        rows = slice(start, start + BLOCK)
        part = lax.dot_general(first, own_ref[rows, :], dims, preferred_element_type=jnp.float32)
        part += lax.dot_general(second, other_ref[rows, :], dims, preferred_element_type=jnp.float32)
        da[:, rows] = part
    inverse, normed = norm_of(xs[slot].astype(jnp.float32))
    d_norm = da[...]
    mean = jnp.mean(d_norm * normed, axis=-1, keepdims=True)
    g_out[...] = (g_ref[...].astype(jnp.float32) + inverse * (d_norm - normed * mean)).astype(jnp.bfloat16)


def forward_body(meta, x_ref, own_ref, other_ref, keep_x, keep_z, keep_a, x_out, xs, zs, acts):
    del keep_x, keep_z, keep_a
    forward_part(meta, x_ref, own_ref, other_ref, x_out, xs, zs, acts)


def backward_body(meta, g_ref, own_ref, other_ref, xs, zs, keep_d, g_out, dzs, da):
    del keep_d
    backward_part(meta, g_ref, own_ref, other_ref, xs, zs, g_out, dzs, da)


def turn_body(
    meta, x_ref, g_ref, own_ref, other_ref, keep_x, keep_z, keep_a, keep_d, x_out, g_out, xs, zs, acts, dzs, da
):
    del keep_x, keep_z, keep_a, keep_d
    forward_part(meta, x_ref, own_ref, other_ref, x_out, xs, zs, acts)
    backward_part(meta, g_ref, own_ref, other_ref, xs, zs, g_out, dzs, da)


VMEM = pl.BlockSpec(memory_space=pltpu.VMEM)
SMEM = pl.BlockSpec(memory_space=pltpu.SMEM)


def run(body, name, meta, free, weights, kept, read, scratch):
    operands = (meta, *free, *weights, *read, *kept)
    first = len(operands) - len(kept)
    return pl.pallas_call(
        body,
        out_shape=tuple(jax.ShapeDtypeStruct(v.shape, v.dtype) for v in free)
        + tuple(pltpu.VMEM(v.shape, v.dtype) for v in kept),
        in_specs=[SMEM] + [VMEM] * (len(operands) - 1),
        out_specs=tuple(VMEM for _ in range(len(free) + len(kept))),
        scratch_shapes=scratch,
        input_output_aliases={first + i: len(free) + i for i in range(len(kept))},
        compiler_params=pltpu.CompilerParams(vmem_limit_bytes=LIMIT),
        name=name,
    )(*operands)


def advanced(values, hours):
    length = values.shape[-2]
    padded = jnp.concatenate([values, jnp.zeros_like(values)], axis=-2)
    return lax.dynamic_slice_in_dim(padded, hours, length, axis=values.ndim - 2)


def shards(features, index, table, exponent, weights, cotangent):
    here = lax.axis_index("section")
    micro, _, length, width = features.shape
    hours = jnp.left_shift(jnp.int32(1), exponent[0])
    onehot = (index[:, :, None] == jnp.arange(table.shape[0], dtype=jnp.int32)).astype(jnp.bfloat16)
    bias = jnp.einsum("mwb,bc->mwc", onehot, table, preferred_element_type=jnp.float32)
    inputs = (features.astype(jnp.float32) + bias[:, :, None, :]).astype(jnp.bfloat16)[:, 0]
    upstream = cotangent[:, 0]
    core = lax.axis_index("core")
    tap = weights[0]
    copies = jnp.broadcast_to(tap[None], (ACROSS,) + tap.shape).reshape(ACROSS * CORES * OWN, width)
    row = lax.all_to_all(copies, ROW, 0, 0, tiled=True)
    own = lax.all_gather(row, DEEP, axis=0, tiled=True)
    other = lax.ppermute(own, "core", [(0, 1), (1, 0)])

    ticks = SECTIONS + micro - 1
    slots = (micro + 1, length, width)
    xs = jnp.zeros(slots, jnp.bfloat16)
    acts = jnp.zeros(slots, jnp.bfloat16)
    zs = jnp.zeros(slots, jnp.float32)
    dzs = jnp.zeros(slots, jnp.bfloat16)
    scratch = [pltpu.VMEM((length, width), jnp.float32)]

    def slot_of(order):
        return jnp.where(jnp.logical_and(order >= 0, order < micro), order, micro)

    def meta_of(ahead, behind):
        parts = [slot_of(ahead - here), hours, core, slot_of(behind - (SECTIONS - 1 - here))]
        return jnp.stack(parts).astype(jnp.int32)

    upward = [(i, i + 1) for i in range(SECTIONS - 1)]
    downward = [(i + 1, i) for i in range(SECTIONS - 1)]

    block = inputs[0]
    grad = upstream[0]
    near = settle((own,), inputs) + settle((other,), inputs)
    for tick in range(ticks + SECTIONS - 1):
        behind = tick - (SECTIONS - 1)
        meta = meta_of(tick, behind)
        if 0 < tick < micro:
            block = jnp.where(here == 0, inputs[tick], block)
        if 0 < behind < micro:
            grad = jnp.where(here == SECTIONS - 1, upstream[behind], grad)
        if behind < 0:
            block, xs, zs, acts = run(forward_body, "layer_forward", meta, (block,), near, (xs, zs, acts), (), [])
            lead = block
        elif tick < ticks:
            block, grad, xs, zs, acts, dzs = run(
                turn_body, "layer_turn", meta, (block, grad), near, (xs, zs, acts, dzs), (), scratch
            )
            lead = grad
        else:
            grad, dzs = run(backward_body, "layer_backward", meta, (grad,), near, (dzs,), (xs, zs), scratch)
            lead = grad
        if tick < ticks + SECTIONS - 2:
            near = settle((own, other), lead)
        if tick < ticks - 1:
            block = lax.ppermute(block, "section", upward)
        if 0 <= behind and tick < ticks + SECTIONS - 2:
            grad = lax.ppermute(grad, "section", downward)
        if tick == ticks + 1:
            every, grad = lax.optimization_barrier((every, grad))
            every = lax.all_gather(every, ROW, axis=0, tiled=False)
        if tick == ticks - 1:
            done = acts[:micro]
            depth = lax.axis_index("zl")
            turns = [[(i, (i + k) % LOW) for i in range(LOW)] for k in range(LOW)]
            moved = [done] + [lax.ppermute(done, "zl", turns[k]) for k in range(1, LOW)]
            every = jnp.stack(
                [
                    jnp.where(depth == j, moved[0], jnp.where((depth - j) % LOW == 1, moved[1], moved[2]))
                    for j in range(LOW)
                ]
            )

    members = LOW * ACROSS * CORES
    piece = width // members
    rows = micro * length
    mine = dzs[:micro].reshape(rows, members, piece).transpose(1, 0, 2)
    theirs = lax.all_to_all(mine, ROW + ("zl",), 0, 0, tiled=True)
    theirs = theirs.reshape(members * micro, length, piece)
    sides = jnp.concatenate([theirs, advanced(theirs, hours)], axis=-1).reshape(members * rows, 2 * piece)
    partial = lax.dot_general(
        every.reshape(members * rows, width), sides, (((0,), (0,)), ((), ())), preferred_element_type=jnp.float32
    ).astype(jnp.bfloat16)
    spread = lax.all_to_all(partial, SHARD, 0, 0, tiled=True)
    back = jnp.sum(spread.reshape(HIGH, LOW, ACROSS * CORES, OWN, 2, piece).astype(jnp.float32), axis=0)
    owned = back.transpose(3, 2, 1, 0, 4).reshape(2, OWN, width)
    return owned[None]


def solution(mesh):
    fine = Mesh(mesh.devices.reshape(SECTIONS, HIGH, LOW, ACROSS, CORES), ("section",) + SHARD)
    placed = (
        P(None, SHARD, None, None),
        P(None, SHARD),
        P(),
        P("section"),
        P("section", None, SHARD, None),
        P(None, SHARD, None, None),
    )
    return jax.shard_map(
        shards, mesh=fine, in_specs=placed, out_specs=P("section", None, SHARD, None), check_vma=False
    )
```

```python
import jax
import jax.numpy as jnp
from jax import lax
from jax.experimental import pallas as pl
from jax.experimental.pallas import tpu as pltpu
from jax.sharding import Mesh, PartitionSpec as P

SECTIONS, HIGH, LOW, ACROSS, CORES = 8, 4, 3, 4, 2
OWN = 16
BLOCK = 256
CHUNKS = 4
LIMIT = 20 * 1024 * 1024
SHARD = ("zh", "zl", "x", "core")
DEEP = ("zh", "zl")
ROW = ("x", "core")
WIDE = ("zl", "x", "core")


def shifted(values, hours, limit_low):
    length = values.shape[0]
    row = lax.broadcasted_iota(jnp.int32, values.shape, 0)
    if limit_low:
        return jnp.where(row >= hours, pltpu.roll(values, hours, 0), 0.0)
    return jnp.where(row < length - hours, pltpu.roll(values, length - hours, 0), 0.0)


def norm_of(x_full):
    inverse = lax.rsqrt(jnp.mean(x_full * x_full, axis=-1, keepdims=True) + 1e-06)
    return inverse, x_full * inverse


def settle_body(*refs):
    count = (len(refs) - 2) // 2
    sems = refs[-1]
    copies = [
        pltpu.make_async_copy(refs[i], refs[count + 1 + i], sems.at[i]) for i in range(count)
    ]
    for copy in copies:
        copy.start()
    for copy in copies:
        copy.wait()


def settle(arrays, after):
    size = sum(v.size * v.dtype.itemsize for v in arrays)
    return pl.pallas_call(
        settle_body,
        out_shape=tuple(pltpu.VMEM(v.shape, v.dtype) for v in arrays),
        in_specs=[pl.BlockSpec(memory_space=pltpu.HBM)] * len(arrays) + [pl.BlockSpec(memory_space=pl.ANY)],
        out_specs=tuple(VMEM for _ in arrays),
        scratch_shapes=[pltpu.SemaphoreType.DMA((len(arrays),))],
        cost_estimate=pl.CostEstimate(flops=0, transcendentals=0, bytes_accessed=4 * size),
        compiler_params=pltpu.CompilerParams(vmem_limit_bytes=LIMIT),
        name="settle",
    )(*(pltpu.with_memory_space_constraint(v, pltpu.HBM) for v in arrays), after)


def ordered(meta, current, moved):
    even = meta[2] == 0
    first = jnp.where(even, current, moved).astype(jnp.bfloat16)
    second = jnp.where(even, moved, current).astype(jnp.bfloat16)
    return first, second


def forward_part(meta, x_ref, own_ref, other_ref, x_out, xs, zs, acts):
    slot = meta[0]
    x_full = x_ref[...].astype(jnp.float32)
    _, normed = norm_of(x_full)
    rounded = normed.astype(jnp.bfloat16)
    xs[slot] = x_ref[...]
    acts[slot] = rounded
    current = rounded.astype(jnp.float32)
    first, second = ordered(meta, current, shifted(current, meta[1], True))
    for start in range(0, x_ref.shape[1], BLOCK):
        cols = slice(start, start + BLOCK)
        pre = jnp.dot(first, own_ref[:, cols], preferred_element_type=jnp.float32)
        pre += jnp.dot(second, other_ref[:, cols], preferred_element_type=jnp.float32)
        zs[slot, :, cols] = pre
        x_out[:, cols] = (x_ref[:, cols].astype(jnp.float32) + pre * jax.nn.sigmoid(pre)).astype(jnp.bfloat16)


def backward_part(meta, g_ref, own_ref, other_ref, xs, zs, g_out, dzs, da):
    slot = meta[3]
    pre = zs[slot]
    sigma = jax.nn.sigmoid(pre)
    d_pre = g_ref[...].astype(jnp.float32) * sigma * (1.0 + pre * (1.0 - sigma))
    d_pre = d_pre.astype(jnp.bfloat16)
    dzs[slot] = d_pre
    current = d_pre.astype(jnp.float32)
    first, second = ordered(meta, current, shifted(current, meta[1], False))
    dims = (((1,), (1,)), ((), ()))
    for start in range(0, g_ref.shape[1], BLOCK):
        rows = slice(start, start + BLOCK)
        part = lax.dot_general(first, own_ref[rows, :], dims, preferred_element_type=jnp.float32)
        part += lax.dot_general(second, other_ref[rows, :], dims, preferred_element_type=jnp.float32)
        da[:, rows] = part
    inverse, normed = norm_of(xs[slot].astype(jnp.float32))
    d_norm = da[...]
    mean = jnp.mean(d_norm * normed, axis=-1, keepdims=True)
    g_out[...] = (g_ref[...].astype(jnp.float32) + inverse * (d_norm - normed * mean)).astype(jnp.bfloat16)


def forward_body(meta, x_ref, own_ref, other_ref, keep_x, keep_z, keep_a, x_out, xs, zs, acts):
    del keep_x, keep_z, keep_a
    forward_part(meta, x_ref, own_ref, other_ref, x_out, xs, zs, acts)


def backward_body(meta, g_ref, own_ref, other_ref, xs, zs, keep_d, g_out, dzs, da):
    del keep_d
    backward_part(meta, g_ref, own_ref, other_ref, xs, zs, g_out, dzs, da)


def last_body(meta, g_ref, own_ref, other_ref, xs, zs, keep_d, g_out, turned, dzs, da):
    backward_body(meta, g_ref, own_ref, other_ref, xs, zs, keep_d, g_out, dzs, da)
    hours_all = jnp.concatenate([dzs[i].astype(jnp.float32) for i in range(dzs.shape[0] - 1)], axis=0)
    turned[...] = hours_all.T.astype(jnp.bfloat16)


def weights_body(meta, turned, source_ref, out, every, sides, total, sems):
    depth = every.shape[0] // CHUNKS
    copies = []
    for index in range(CHUNKS):
        span = slice(index * depth, (index + 1) * depth)
        copies.append(pltpu.make_async_copy(source_ref.at[span], every.at[span], sems.at[index]))
        copies[-1].start()
    members = every.shape[0] // turned.shape[1]
    piece = turned.shape[0] // members
    length = turned.shape[1] // 2
    hours = meta[1]
    current = turned[...].astype(jnp.float32)
    lane = lax.broadcasted_iota(jnp.int32, current.shape, 1) % length
    moved = jnp.where(lane < length - hours, pltpu.roll(current, 2 * length - hours, 1), 0.0)
    for source in range(members):
        span = slice(source * piece, (source + 1) * piece)
        lanes = slice(source * 2 * length, (source + 1) * 2 * length)
        sides[:piece, lanes] = current[span].astype(jnp.bfloat16)
        sides[piece:, lanes] = moved[span].astype(jnp.bfloat16)
    chips = BLOCK // (CORES * OWN)
    for index in range(CHUNKS):
        copies[index].wait()
        span = slice(index * depth, (index + 1) * depth)
        for block, start in enumerate(range(0, every.shape[1], BLOCK)):
            cols = slice(start, start + BLOCK)
            part = jnp.dot(sides[:, span], every[span, cols], preferred_element_type=jnp.float32)
            if index > 0:
                part += total[:, cols]
            if index < CHUNKS - 1:
                total[:, cols] = part
                continue
            part = part.T.reshape(chips, CORES, OWN, 2 * piece).astype(jnp.bfloat16)
            for core in range(CORES):
                out[core, block * chips : (block + 1) * chips] = part[:, core]


def weight_partials(meta, turned, every):
    tokens, width = every.shape
    piece = width * turned.shape[1] // tokens
    return pl.pallas_call(
        weights_body,
        out_shape=jax.ShapeDtypeStruct((CORES, width // (CORES * OWN), OWN, 2 * piece), jnp.bfloat16),
        in_specs=[SMEM, VMEM, pl.BlockSpec(memory_space=pltpu.HBM)],
        out_specs=VMEM,
        scratch_shapes=[
            pltpu.VMEM(every.shape, every.dtype),
            pltpu.VMEM((2 * piece, tokens), jnp.bfloat16),
            pltpu.VMEM((2 * piece, width), jnp.float32),
            pltpu.SemaphoreType.DMA((CHUNKS,)),
        ],
        compiler_params=pltpu.CompilerParams(vmem_limit_bytes=LIMIT),
        name="weight_partials",
    )(meta, turned, pltpu.with_memory_space_constraint(every, pltpu.HBM))


def turn_body(
    meta, x_ref, g_ref, own_ref, other_ref, keep_x, keep_z, keep_a, keep_d, x_out, g_out, xs, zs, acts, dzs, da
):
    del keep_x, keep_z, keep_a, keep_d
    forward_part(meta, x_ref, own_ref, other_ref, x_out, xs, zs, acts)
    backward_part(meta, g_ref, own_ref, other_ref, xs, zs, g_out, dzs, da)


VMEM = pl.BlockSpec(memory_space=pltpu.VMEM)
SMEM = pl.BlockSpec(memory_space=pltpu.SMEM)


def run(body, name, meta, free, weights, kept, read, scratch, extra=()):
    operands = (meta, *free, *weights, *read, *kept)
    first = len(operands) - len(kept)
    return pl.pallas_call(
        body,
        out_shape=tuple(jax.ShapeDtypeStruct(v.shape, v.dtype) for v in (*free, *extra))
        + tuple(pltpu.VMEM(v.shape, v.dtype) for v in kept),
        in_specs=[SMEM] + [VMEM] * (len(operands) - 1),
        out_specs=tuple(VMEM for _ in range(len(free) + len(extra) + len(kept))),
        scratch_shapes=scratch,
        input_output_aliases={first + i: len(free) + len(extra) + i for i in range(len(kept))},
        compiler_params=pltpu.CompilerParams(vmem_limit_bytes=LIMIT),
        name=name,
    )(*operands)


def shards(features, index, table, exponent, weights, cotangent):
    here = lax.axis_index("section")
    micro, _, length, width = features.shape
    hours = jnp.left_shift(jnp.int32(1), exponent[0])
    onehot = (index[:, :, None] == jnp.arange(table.shape[0], dtype=jnp.int32)).astype(jnp.bfloat16)
    bias = jnp.einsum("mwb,bc->mwc", onehot, table, preferred_element_type=jnp.float32)
    inputs = (features.astype(jnp.float32) + bias[:, :, None, :]).astype(jnp.bfloat16)[:, 0]
    upstream = cotangent[:, 0]
    core = lax.axis_index("core")
    tap = weights[0]
    copies = jnp.broadcast_to(tap[None], (ACROSS,) + tap.shape).reshape(ACROSS * CORES * OWN, width)
    row = lax.all_to_all(copies, ROW, 0, 0, tiled=True)
    own = lax.all_gather(row, DEEP, axis=0, tiled=True)
    other = lax.ppermute(own, "core", [(0, 1), (1, 0)])

    ticks = SECTIONS + micro - 1
    slots = (micro + 1, length, width)
    xs = jnp.zeros(slots, jnp.bfloat16)
    acts = jnp.zeros(slots, jnp.bfloat16)
    zs = jnp.zeros(slots, jnp.float32)
    dzs = jnp.zeros(slots, jnp.bfloat16)
    scratch = [pltpu.VMEM((length, width), jnp.float32)]

    def slot_of(order):
        return jnp.where(jnp.logical_and(order >= 0, order < micro), order, micro)

    def meta_of(ahead, behind):
        parts = [slot_of(ahead - here), hours, core, slot_of(behind - (SECTIONS - 1 - here))]
        return jnp.stack(parts).astype(jnp.int32)

    upward = [(i, i + 1) for i in range(SECTIONS - 1)]
    downward = [(i + 1, i) for i in range(SECTIONS - 1)]

    block = inputs[0]
    grad = upstream[0]
    near = settle((own,), inputs) + settle((other,), inputs)
    for tick in range(ticks + SECTIONS - 1):
        behind = tick - (SECTIONS - 1)
        meta = meta_of(tick, behind)
        if 0 < tick < micro:
            block = jnp.where(here == 0, inputs[tick], block)
        if 0 < behind < micro:
            grad = jnp.where(here == SECTIONS - 1, upstream[behind], grad)
        if behind < 0:
            block, xs, zs, acts = run(forward_body, "layer_forward", meta, (block,), near, (xs, zs, acts), (), [])
            lead = block
        elif tick < ticks:
            block, grad, xs, zs, acts, dzs = run(
                turn_body, "layer_turn", meta, (block, grad), near, (xs, zs, acts, dzs), (), scratch
            )
            lead = grad
        elif tick == ticks + SECTIONS - 2:
            turned = jax.ShapeDtypeStruct((width, micro * length), jnp.bfloat16)
            grad, turned, dzs = run(
                last_body, "layer_last", meta, (grad,), near, (dzs,), (xs, zs), scratch, (turned,)
            )
        else:
            grad, dzs = run(backward_body, "layer_backward", meta, (grad,), near, (dzs,), (xs, zs), scratch)
            lead = grad
        if tick < ticks + SECTIONS - 2:
            near = settle((own, other), lead)
        if tick < ticks - 1:
            block = lax.ppermute(block, "section", upward)
        if 0 <= behind and tick < ticks + SECTIONS - 2:
            grad = lax.ppermute(grad, "section", downward)
        if tick == ticks + 1:
            every, grad = lax.optimization_barrier((every, grad))
            every = lax.all_gather(every, ROW, axis=0, tiled=False)
        if tick == ticks - 1:
            done = acts[:micro]
            depth = lax.axis_index("zl")
            turns = [[(i, (i + k) % LOW) for i in range(LOW)] for k in range(LOW)]
            moved = [done] + [lax.ppermute(done, "zl", turns[k]) for k in range(1, LOW)]
            every = jnp.stack(
                [
                    jnp.where(depth == j, moved[0], jnp.where((depth - j) % LOW == 1, moved[1], moved[2]))
                    for j in range(LOW)
                ]
            )

    members = LOW * ACROSS * CORES
    piece = width // members
    theirs = lax.all_to_all(turned, ROW + ("zl",), 0, 0, tiled=True)
    partial = weight_partials(meta, theirs, every.reshape(members * micro * length, width))
    both = lax.all_to_all(partial, "core", 0, 0, tiled=True).transpose(1, 0, 2, 3)
    spread = lax.all_to_all(both, DEEP + ("x",), 0, 0, tiled=True)
    back = jnp.sum(spread.reshape(HIGH, members * OWN, 2 * piece).astype(jnp.float32), axis=0)
    back = back.reshape(LOW, ACROSS * CORES, OWN, 2, piece)
    owned = back.transpose(3, 2, 1, 0, 4).reshape(2, OWN, width)
    return owned[None]


def solution(mesh):
    fine = Mesh(mesh.devices.reshape(SECTIONS, HIGH, LOW, ACROSS, CORES), ("section",) + SHARD)
    placed = (
        P(None, SHARD, None, None),
        P(None, SHARD),
        P(),
        P("section"),
        P("section", None, SHARD, None),
        P(None, SHARD, None, None),
    )
    return jax.shard_map(
        shards, mesh=fine, in_specs=placed, out_specs=P("section", None, SHARD, None), check_vma=False
    )
```

```python
import jax
import jax.numpy as jnp
from jax import lax
from jax.experimental import pallas as pl
from jax.experimental.pallas import tpu as pltpu
from jax.sharding import Mesh, PartitionSpec as P

SECTIONS, HIGH, LOW, ACROSS, CORES = 8, 4, 3, 4, 2
OWN = 16
BLOCK = 256
CHUNKS = 4
NEAR = 768
LIMIT = 20 * 1024 * 1024
SHARD = ("zh", "zl", "x", "core")
DEEP = ("zh", "zl")
ROW = ("x", "core")
WIDE = ("zl", "x", "core")


def shifted(values, hours, limit_low):
    length = values.shape[0]
    row = lax.broadcasted_iota(jnp.int32, values.shape, 0)
    if limit_low:
        return jnp.where(row >= hours, pltpu.roll(values, hours, 0), 0.0)
    return jnp.where(row < length - hours, pltpu.roll(values, length - hours, 0), 0.0)


def norm_of(x_full):
    inverse = lax.rsqrt(jnp.mean(x_full * x_full, axis=-1, keepdims=True) + 1e-06)
    return inverse, x_full * inverse


def settle_body(*refs):
    count = (len(refs) - 2) // 2
    sems = refs[-1]
    copies = []
    for i in range(count):
        source, target = refs[i], refs[count + 1 + i]
        if source.shape != target.shape:
            source = source.at[:, : target.shape[1]]
        copies.append(pltpu.make_async_copy(source, target, sems.at[i]))
    for copy in copies:
        copy.start()
    for copy in copies:
        copy.wait()


def settle(arrays, after, widths=None):
    size = sum(v.size * v.dtype.itemsize for v in arrays)
    return pl.pallas_call(
        settle_body,
        out_shape=tuple(
            pltpu.VMEM((v.shape[0], w), v.dtype) for v, w in zip(arrays, widths or [v.shape[1] for v in arrays])
        ),
        in_specs=[pl.BlockSpec(memory_space=pltpu.HBM)] * len(arrays) + [pl.BlockSpec(memory_space=pl.ANY)],
        out_specs=tuple(VMEM for _ in arrays),
        scratch_shapes=[pltpu.SemaphoreType.DMA((len(arrays),))],
        cost_estimate=pl.CostEstimate(flops=0, transcendentals=0, bytes_accessed=4 * size),
        compiler_params=pltpu.CompilerParams(vmem_limit_bytes=LIMIT),
        name="settle",
    )(*(pltpu.with_memory_space_constraint(v, pltpu.HBM) for v in arrays), after)


def ordered(meta, current, moved):
    even = meta[2] == 0
    first = jnp.where(even, current, moved).astype(jnp.bfloat16)
    second = jnp.where(even, moved, current).astype(jnp.bfloat16)
    return first, second


def forward_part(meta, x_ref, own_ref, other_ref, x_out, xs, zs, acts, rest=None):
    slot = meta[0]
    near = other_ref.shape[1]
    if rest is not None:
        far_ref, buffer, sem = rest
        fetch = pltpu.make_async_copy(far_ref.at[:, near:], buffer, sem)
        fetch.start()
    x_full = x_ref[...].astype(jnp.float32)
    _, normed = norm_of(x_full)
    rounded = normed.astype(jnp.bfloat16)
    xs[slot] = x_ref[...]
    acts[slot] = rounded
    current = rounded.astype(jnp.float32)
    first, second = ordered(meta, current, shifted(current, meta[1], True))
    for start in range(0, x_ref.shape[1], BLOCK):
        cols = slice(start, start + BLOCK)
        pre = jnp.dot(first, own_ref[:, cols], preferred_element_type=jnp.float32)
        if start == near:
            fetch.wait()
        if start < near:
            tile = other_ref[:, cols]
        else:
            tile = buffer[:, start - near : start - near + BLOCK]
        pre += jnp.dot(second, tile, preferred_element_type=jnp.float32)
        zs[slot, :, cols] = pre
        x_out[:, cols] = (x_ref[:, cols].astype(jnp.float32) + pre * jax.nn.sigmoid(pre)).astype(jnp.bfloat16)


def backward_part(meta, g_ref, own_ref, other_ref, xs, zs, g_out, dzs, da):
    slot = meta[3]
    pre = zs[slot]
    sigma = jax.nn.sigmoid(pre)
    d_pre = g_ref[...].astype(jnp.float32) * sigma * (1.0 + pre * (1.0 - sigma))
    d_pre = d_pre.astype(jnp.bfloat16)
    dzs[slot] = d_pre
    current = d_pre.astype(jnp.float32)
    first, second = ordered(meta, current, shifted(current, meta[1], False))
    dims = (((1,), (1,)), ((), ()))
    for start in range(0, g_ref.shape[1], BLOCK):
        rows = slice(start, start + BLOCK)
        part = lax.dot_general(first, own_ref[rows, :], dims, preferred_element_type=jnp.float32)
        part += lax.dot_general(second, other_ref[rows, :], dims, preferred_element_type=jnp.float32)
        da[:, rows] = part
    inverse, normed = norm_of(xs[slot].astype(jnp.float32))
    d_norm = da[...]
    mean = jnp.mean(d_norm * normed, axis=-1, keepdims=True)
    g_out[...] = (g_ref[...].astype(jnp.float32) + inverse * (d_norm - normed * mean)).astype(jnp.bfloat16)


def forward_body(
    meta, x_ref, own_ref, other_ref, far_ref, keep_x, keep_z, keep_a, x_out, xs, zs, acts, buffer, sem
):
    del keep_x, keep_z, keep_a
    forward_part(meta, x_ref, own_ref, other_ref, x_out, xs, zs, acts, (far_ref, buffer, sem))


def backward_body(meta, g_ref, own_ref, other_ref, xs, zs, keep_d, g_out, dzs, da):
    del keep_d
    backward_part(meta, g_ref, own_ref, other_ref, xs, zs, g_out, dzs, da)


def last_body(meta, g_ref, own_ref, other_ref, xs, zs, keep_d, g_out, turned, dzs, da):
    backward_body(meta, g_ref, own_ref, other_ref, xs, zs, keep_d, g_out, dzs, da)
    hours_all = jnp.concatenate([dzs[i].astype(jnp.float32) for i in range(dzs.shape[0] - 1)], axis=0)
    turned[...] = hours_all.T.astype(jnp.bfloat16)


def weights_body(meta, turned, source_ref, out, every, sides, total, sems):
    depth = every.shape[0] // CHUNKS
    copies = []
    for index in range(CHUNKS):
        span = slice(index * depth, (index + 1) * depth)
        copies.append(pltpu.make_async_copy(source_ref.at[span], every.at[span], sems.at[index]))
        copies[-1].start()
    members = every.shape[0] // turned.shape[1]
    piece = turned.shape[0] // members
    length = turned.shape[1] // 2
    hours = meta[1]
    current = turned[...].astype(jnp.float32)
    lane = lax.broadcasted_iota(jnp.int32, current.shape, 1) % length
    moved = jnp.where(lane < length - hours, pltpu.roll(current, 2 * length - hours, 1), 0.0)
    for source in range(members):
        span = slice(source * piece, (source + 1) * piece)
        lanes = slice(source * 2 * length, (source + 1) * 2 * length)
        sides[:piece, lanes] = current[span].astype(jnp.bfloat16)
        sides[piece:, lanes] = moved[span].astype(jnp.bfloat16)
    for index in range(CHUNKS):
        copies[index].wait()
        span = slice(index * depth, (index + 1) * depth)
        for start in range(0, every.shape[1], BLOCK):
            cols = slice(start, start + BLOCK)
            part = jnp.dot(sides[:, span], every[span, cols], preferred_element_type=jnp.float32)
            if index > 0:
                part += total[:, cols]
            if index < CHUNKS - 1:
                total[:, cols] = part
                continue
            out[cols, :] = part.T.astype(jnp.bfloat16)


def weight_partials(meta, turned, every):
    tokens, width = every.shape
    piece = width * turned.shape[1] // tokens
    return pl.pallas_call(
        weights_body,
        out_shape=jax.ShapeDtypeStruct((width, 2 * piece), jnp.bfloat16),
        in_specs=[SMEM, VMEM, pl.BlockSpec(memory_space=pltpu.HBM)],
        out_specs=VMEM,
        scratch_shapes=[
            pltpu.VMEM(every.shape, every.dtype),
            pltpu.VMEM((2 * piece, tokens), jnp.bfloat16),
            pltpu.VMEM((2 * piece, width), jnp.float32),
            pltpu.SemaphoreType.DMA((CHUNKS,)),
        ],
        compiler_params=pltpu.CompilerParams(vmem_limit_bytes=LIMIT),
        name="weight_partials",
    )(meta, turned, pltpu.with_memory_space_constraint(every, pltpu.HBM))


def turn_body(
    meta, x_ref, g_ref, own_ref, other_ref, keep_x, keep_z, keep_a, keep_d, x_out, g_out, xs, zs, acts, dzs, da
):
    del keep_x, keep_z, keep_a, keep_d
    forward_part(meta, x_ref, own_ref, other_ref, x_out, xs, zs, acts)
    backward_part(meta, g_ref, own_ref, other_ref, xs, zs, g_out, dzs, da)


VMEM = pl.BlockSpec(memory_space=pltpu.VMEM)
SMEM = pl.BlockSpec(memory_space=pltpu.SMEM)
HBM = pl.BlockSpec(memory_space=pltpu.HBM)


def run(body, name, meta, free, weights, kept, read, scratch, extra=(), far=None):
    operands = (meta, *free, *weights, *read, *kept)
    first = len(operands) - len(kept)
    return pl.pallas_call(
        body,
        out_shape=tuple(jax.ShapeDtypeStruct(v.shape, v.dtype) for v in (*free, *extra))
        + tuple(pltpu.VMEM(v.shape, v.dtype) for v in kept),
        in_specs=[SMEM]
        + [VMEM] * (len(free) + len(weights))
        + [far or VMEM] * len(read)
        + [VMEM] * len(kept),
        out_specs=tuple(VMEM for _ in range(len(free) + len(extra) + len(kept))),
        scratch_shapes=scratch,
        input_output_aliases={first + i: len(free) + len(extra) + i for i in range(len(kept))},
        compiler_params=pltpu.CompilerParams(vmem_limit_bytes=LIMIT),
        name=name,
    )(*operands)


def shards(features, index, table, exponent, weights, cotangent):
    here = lax.axis_index("section")
    micro, _, length, width = features.shape
    hours = jnp.left_shift(jnp.int32(1), exponent[0])
    onehot = (index[:, :, None] == jnp.arange(table.shape[0], dtype=jnp.int32)).astype(jnp.bfloat16)
    bias = jnp.einsum("mwb,bc->mwc", onehot, table, preferred_element_type=jnp.float32)
    inputs = (features.astype(jnp.float32) + bias[:, :, None, :]).astype(jnp.bfloat16)[:, 0]
    upstream = cotangent[:, 0]
    core = lax.axis_index("core")
    tap = weights[0]
    copies = jnp.broadcast_to(tap[None], (ACROSS,) + tap.shape).reshape(ACROSS * CORES * OWN, width)
    row = lax.all_to_all(copies, ROW, 0, 0, tiled=True)
    own = lax.all_gather(row, DEEP, axis=0, tiled=True)
    other = lax.ppermute(own, "core", [(0, 1), (1, 0)])

    ticks = SECTIONS + micro - 1
    slots = (micro + 1, length, width)
    xs = jnp.zeros(slots, jnp.bfloat16)
    acts = jnp.zeros(slots, jnp.bfloat16)
    zs = jnp.zeros(slots, jnp.float32)
    dzs = jnp.zeros(slots, jnp.bfloat16)
    scratch = [pltpu.VMEM((length, width), jnp.float32)]
    streams = [pltpu.VMEM((width, width - NEAR), jnp.bfloat16), pltpu.SemaphoreType.DMA]

    def slot_of(order):
        return jnp.where(jnp.logical_and(order >= 0, order < micro), order, micro)

    def meta_of(ahead, behind):
        parts = [slot_of(ahead - here), hours, core, slot_of(behind - (SECTIONS - 1 - here))]
        return jnp.stack(parts).astype(jnp.int32)

    upward = [(i, i + 1) for i in range(SECTIONS - 1)]
    downward = [(i + 1, i) for i in range(SECTIONS - 1)]

    block = inputs[0]
    grad = upstream[0]
    near = settle((own,), inputs) + settle((other,), inputs, (NEAR,))
    for tick in range(ticks + SECTIONS - 1):
        behind = tick - (SECTIONS - 1)
        meta = meta_of(tick, behind)
        if 0 < tick < micro:
            block = jnp.where(here == 0, inputs[tick], block)
        if 0 < behind < micro:
            grad = jnp.where(here == SECTIONS - 1, upstream[behind], grad)
        if behind < 0:
            far = pltpu.with_memory_space_constraint(other, pltpu.HBM)
            block, xs, zs, acts = run(
                forward_body, "layer_forward", meta, (block,), near, (xs, zs, acts), (far,), streams, far=HBM
            )
            lead = block
        elif tick < ticks:
            block, grad, xs, zs, acts, dzs = run(
                turn_body, "layer_turn", meta, (block, grad), near, (xs, zs, acts, dzs), (), scratch
            )
            lead = grad
        elif tick == ticks + SECTIONS - 2:
            turned = jax.ShapeDtypeStruct((width, micro * length), jnp.bfloat16)
            grad, turned, dzs = run(
                last_body, "layer_last", meta, (grad,), near, (dzs,), (xs, zs), scratch, (turned,)
            )
        else:
            grad, dzs = run(backward_body, "layer_backward", meta, (grad,), near, (dzs,), (xs, zs), scratch)
            lead = grad
        if tick < ticks + SECTIONS - 2:
            part = NEAR if behind < -1 else width
            near = settle((own, other), lead, (width, part))
        if tick < ticks - 1:
            block = lax.ppermute(block, "section", upward)
        if 0 <= behind and tick < ticks + SECTIONS - 2:
            grad = lax.ppermute(grad, "section", downward)
        if tick == ticks + 1:
            every, grad = lax.optimization_barrier((every, grad))
            every = lax.all_gather(every, ROW, axis=0, tiled=False)
        if tick == ticks - 1:
            done = acts[:micro]
            depth = lax.axis_index("zl")
            turns = [[(i, (i + k) % LOW) for i in range(LOW)] for k in range(LOW)]
            moved = [done] + [lax.ppermute(done, "zl", turns[k]) for k in range(1, LOW)]
            every = jnp.stack(
                [
                    jnp.where(depth == j, moved[0], jnp.where((depth - j) % LOW == 1, moved[1], moved[2]))
                    for j in range(LOW)
                ]
            )

    members = LOW * ACROSS * CORES
    piece = width // members
    theirs = lax.all_to_all(turned, ROW + ("zl",), 0, 0, tiled=True)
    partial = weight_partials(meta, theirs, every.reshape(members * micro * length, width))
    spread = lax.all_to_all(partial, DEEP, 0, 0, tiled=True)
    total = jnp.sum(spread.reshape(HIGH, LOW * ACROSS * CORES * OWN, 2 * piece).astype(jnp.float32), axis=0)
    total = total.reshape(LOW, ACROSS * CORES, OWN, 2 * piece).transpose(1, 0, 2, 3)
    back = lax.all_to_all(total, ROW, 0, 0, tiled=True).reshape(ACROSS * CORES, LOW, OWN, 2, piece)
    owned = back.transpose(3, 2, 0, 1, 4).reshape(2, OWN, width)
    return owned[None]


def solution(mesh):
    fine = Mesh(mesh.devices.reshape(SECTIONS, HIGH, LOW, ACROSS, CORES), ("section",) + SHARD)
    placed = (
        P(None, SHARD, None, None),
        P(None, SHARD),
        P(),
        P("section"),
        P("section", None, SHARD, None),
        P(None, SHARD, None, None),
    )
    return jax.shard_map(
        shards, mesh=fine, in_specs=placed, out_specs=P("section", None, SHARD, None), check_vma=False
    )
```

```python
import jax
import jax.numpy as jnp
from jax import lax
from jax.experimental import pallas as pl
from jax.experimental.pallas import tpu as pltpu
from jax.sharding import Mesh, PartitionSpec as P

SECTIONS, HIGH, LOW, ACROSS, CORES = 8, 4, 3, 4, 2
OWN = 16
BLOCK = 256
CHUNKS = 4
LIMIT = 20 * 1024 * 1024
SHARD = ("zh", "zl", "x", "core")
DEEP = ("zh", "zl")
ROW = ("x", "core")
WIDE = ("zl", "x", "core")


def shifted(values, hours, limit_low):
    length = values.shape[0]
    row = lax.broadcasted_iota(jnp.int32, values.shape, 0)
    if limit_low:
        return jnp.where(row >= hours, pltpu.roll(values, hours, 0), 0.0)
    return jnp.where(row < length - hours, pltpu.roll(values, length - hours, 0), 0.0)


def norm_of(x_full):
    inverse = lax.rsqrt(jnp.mean(x_full * x_full, axis=-1, keepdims=True) + 1e-06)
    return inverse, x_full * inverse


def settle_body(*refs):
    count = (len(refs) - 2) // 2
    sems = refs[-1]
    copies = [
        pltpu.make_async_copy(refs[i], refs[count + 1 + i], sems.at[i]) for i in range(count)
    ]
    for copy in copies:
        copy.start()
    for copy in copies:
        copy.wait()


def settle(arrays, after):
    size = sum(v.size * v.dtype.itemsize for v in arrays)
    return pl.pallas_call(
        settle_body,
        out_shape=tuple(pltpu.VMEM(v.shape, v.dtype) for v in arrays),
        in_specs=[pl.BlockSpec(memory_space=pltpu.HBM)] * len(arrays) + [pl.BlockSpec(memory_space=pl.ANY)],
        out_specs=tuple(VMEM for _ in arrays),
        scratch_shapes=[pltpu.SemaphoreType.DMA((len(arrays),))],
        cost_estimate=pl.CostEstimate(flops=0, transcendentals=0, bytes_accessed=4 * size),
        compiler_params=pltpu.CompilerParams(vmem_limit_bytes=LIMIT),
        name="settle",
    )(*(pltpu.with_memory_space_constraint(v, pltpu.HBM) for v in arrays), after)


def ordered(meta, current, moved):
    even = meta[2] == 0
    first = jnp.where(even, current, moved).astype(jnp.bfloat16)
    second = jnp.where(even, moved, current).astype(jnp.bfloat16)
    return first, second


def forward_part(meta, x_ref, own_ref, other_ref, x_out, xs, zs, acts):
    slot = meta[0]
    x_full = x_ref[...].astype(jnp.float32)
    _, normed = norm_of(x_full)
    rounded = normed.astype(jnp.bfloat16)
    xs[slot] = x_ref[...]
    acts[slot] = rounded
    current = rounded.astype(jnp.float32)
    first, second = ordered(meta, current, shifted(current, meta[1], True))
    for start in range(0, x_ref.shape[1], BLOCK):
        cols = slice(start, start + BLOCK)
        pre = jnp.dot(first, own_ref[:, cols], preferred_element_type=jnp.float32)
        pre += jnp.dot(second, other_ref[:, cols], preferred_element_type=jnp.float32)
        zs[slot, :, cols] = pre
        x_out[:, cols] = (x_ref[:, cols].astype(jnp.float32) + pre * jax.nn.sigmoid(pre)).astype(jnp.bfloat16)


def backward_part(meta, g_ref, own_ref, other_ref, xs, zs, g_out, dzs, da):
    slot = meta[3]
    pre = zs[slot]
    sigma = jax.nn.sigmoid(pre)
    d_pre = g_ref[...].astype(jnp.float32) * sigma * (1.0 + pre * (1.0 - sigma))
    d_pre = d_pre.astype(jnp.bfloat16)
    dzs[slot] = d_pre
    current = d_pre.astype(jnp.float32)
    first, second = ordered(meta, current, shifted(current, meta[1], False))
    dims = (((1,), (1,)), ((), ()))
    for start in range(0, g_ref.shape[1], BLOCK):
        rows = slice(start, start + BLOCK)
        part = lax.dot_general(first, own_ref[rows, :], dims, preferred_element_type=jnp.float32)
        part += lax.dot_general(second, other_ref[rows, :], dims, preferred_element_type=jnp.float32)
        da[:, rows] = part
    inverse, normed = norm_of(xs[slot].astype(jnp.float32))
    d_norm = da[...]
    mean = jnp.mean(d_norm * normed, axis=-1, keepdims=True)
    g_out[...] = (g_ref[...].astype(jnp.float32) + inverse * (d_norm - normed * mean)).astype(jnp.bfloat16)


def forward_body(meta, x_ref, own_ref, other_ref, keep_x, keep_z, keep_a, x_out, xs, zs, acts):
    del keep_x, keep_z, keep_a
    forward_part(meta, x_ref, own_ref, other_ref, x_out, xs, zs, acts)


def backward_body(meta, g_ref, own_ref, other_ref, xs, zs, keep_d, g_out, dzs, da):
    del keep_d
    backward_part(meta, g_ref, own_ref, other_ref, xs, zs, g_out, dzs, da)


def last_body(meta, g_ref, own_ref, other_ref, xs, zs, keep_d, g_out, turned, dzs, da):
    backward_body(meta, g_ref, own_ref, other_ref, xs, zs, keep_d, g_out, dzs, da)
    hours_all = jnp.concatenate([dzs[i].astype(jnp.float32) for i in range(dzs.shape[0] - 1)], axis=0)
    turned[...] = hours_all.T.astype(jnp.bfloat16)


def weights_body(meta, turned, source_ref, out, every, sides, total, sems):
    depth = every.shape[0] // CHUNKS
    copies = []
    for index in range(CHUNKS):
        span = slice(index * depth, (index + 1) * depth)
        copies.append(pltpu.make_async_copy(source_ref.at[span], every.at[span], sems.at[index]))
        copies[-1].start()
    members = every.shape[0] // turned.shape[1]
    piece = turned.shape[0] // members
    length = turned.shape[1] // 2
    hours = meta[1]
    current = turned[...].astype(jnp.float32)
    lane = lax.broadcasted_iota(jnp.int32, current.shape, 1) % length
    moved = jnp.where(lane < length - hours, pltpu.roll(current, 2 * length - hours, 1), 0.0)
    for source in range(members):
        span = slice(source * piece, (source + 1) * piece)
        lanes = slice(source * 2 * length, (source + 1) * 2 * length)
        sides[:piece, lanes] = current[span].astype(jnp.bfloat16)
        sides[piece:, lanes] = moved[span].astype(jnp.bfloat16)
    for index in range(CHUNKS):
        copies[index].wait()
        span = slice(index * depth, (index + 1) * depth)
        for start in range(0, every.shape[1], BLOCK):
            cols = slice(start, start + BLOCK)
            part = jnp.dot(sides[:, span], every[span, cols], preferred_element_type=jnp.float32)
            if index > 0:
                part += total[:, cols]
            if index < CHUNKS - 1:
                total[:, cols] = part
                continue
            out[cols, :] = part.T.astype(jnp.bfloat16)


def weight_partials(meta, turned, every):
    tokens, width = every.shape
    piece = width * turned.shape[1] // tokens
    return pl.pallas_call(
        weights_body,
        out_shape=jax.ShapeDtypeStruct((width, 2 * piece), jnp.bfloat16),
        in_specs=[SMEM, VMEM, pl.BlockSpec(memory_space=pltpu.HBM)],
        out_specs=VMEM,
        scratch_shapes=[
            pltpu.VMEM(every.shape, every.dtype),
            pltpu.VMEM((2 * piece, tokens), jnp.bfloat16),
            pltpu.VMEM((2 * piece, width), jnp.float32),
            pltpu.SemaphoreType.DMA((CHUNKS,)),
        ],
        compiler_params=pltpu.CompilerParams(vmem_limit_bytes=LIMIT),
        name="weight_partials",
    )(meta, turned, pltpu.with_memory_space_constraint(every, pltpu.HBM))


def turn_body(
    meta, x_ref, g_ref, own_ref, other_ref, keep_x, keep_z, keep_a, keep_d, x_out, g_out, xs, zs, acts, dzs, da
):
    del keep_x, keep_z, keep_a, keep_d
    forward_part(meta, x_ref, own_ref, other_ref, x_out, xs, zs, acts)
    backward_part(meta, g_ref, own_ref, other_ref, xs, zs, g_out, dzs, da)


VMEM = pl.BlockSpec(memory_space=pltpu.VMEM)
SMEM = pl.BlockSpec(memory_space=pltpu.SMEM)


def run(body, name, meta, free, weights, kept, read, scratch, extra=()):
    operands = (meta, *free, *weights, *read, *kept)
    first = len(operands) - len(kept)
    return pl.pallas_call(
        body,
        out_shape=tuple(jax.ShapeDtypeStruct(v.shape, v.dtype) for v in (*free, *extra))
        + tuple(pltpu.VMEM(v.shape, v.dtype) for v in kept),
        in_specs=[SMEM] + [VMEM] * (len(operands) - 1),
        out_specs=tuple(VMEM for _ in range(len(free) + len(extra) + len(kept))),
        scratch_shapes=scratch,
        input_output_aliases={first + i: len(free) + len(extra) + i for i in range(len(kept))},
        compiler_params=pltpu.CompilerParams(vmem_limit_bytes=LIMIT),
        name=name,
    )(*operands)


def shards(features, index, table, exponent, weights, cotangent):
    here = lax.axis_index("section")
    micro, _, length, width = features.shape
    hours = jnp.left_shift(jnp.int32(1), exponent[0])
    onehot = (index[:, :, None] == jnp.arange(table.shape[0], dtype=jnp.int32)).astype(jnp.bfloat16)
    bias = jnp.einsum("mwb,bc->mwc", onehot, table, preferred_element_type=jnp.float32)
    inputs = (features.astype(jnp.float32) + bias[:, :, None, :]).astype(jnp.bfloat16)[:, 0]
    upstream = cotangent[:, 0]
    core = lax.axis_index("core")
    tap = weights[0]
    copies = jnp.broadcast_to(tap[None], (ACROSS,) + tap.shape).reshape(ACROSS * CORES * OWN, width)
    row = lax.all_to_all(copies, ROW, 0, 0, tiled=True)
    own = lax.all_gather(row, DEEP, axis=0, tiled=True)
    other = lax.ppermute(own, "core", [(0, 1), (1, 0)])

    ticks = SECTIONS + micro - 1
    slots = (micro + 1, length, width)
    xs = jnp.zeros(slots, jnp.bfloat16)
    acts = jnp.zeros(slots, jnp.bfloat16)
    zs = jnp.zeros(slots, jnp.float32)
    dzs = jnp.zeros(slots, jnp.bfloat16)
    scratch = [pltpu.VMEM((length, width), jnp.float32)]

    def slot_of(order):
        return jnp.where(jnp.logical_and(order >= 0, order < micro), order, micro)

    def meta_of(ahead, behind):
        parts = [slot_of(ahead - here), hours, core, slot_of(behind - (SECTIONS - 1 - here))]
        return jnp.stack(parts).astype(jnp.int32)

    upward = [(i, i + 1) for i in range(SECTIONS - 1)]
    downward = [(i + 1, i) for i in range(SECTIONS - 1)]

    block = inputs[0]
    grad = upstream[0]
    near = settle((own,), inputs) + settle((other,), inputs)
    for tick in range(ticks + SECTIONS - 1):
        behind = tick - (SECTIONS - 1)
        meta = meta_of(tick, behind)
        if 0 < tick < micro:
            block = jnp.where(here == 0, inputs[tick], block)
        if 0 < behind < micro:
            grad = jnp.where(here == SECTIONS - 1, upstream[behind], grad)
        if behind < 0:
            block, xs, zs, acts = run(forward_body, "layer_forward", meta, (block,), near, (xs, zs, acts), (), [])
            lead = block
        elif tick < ticks:
            block, grad, xs, zs, acts, dzs = run(
                turn_body, "layer_turn", meta, (block, grad), near, (xs, zs, acts, dzs), (), scratch
            )
            lead = grad
        elif tick == ticks + SECTIONS - 2:
            turned = jax.ShapeDtypeStruct((width, micro * length), jnp.bfloat16)
            grad, turned, dzs = run(
                last_body, "layer_last", meta, (grad,), near, (dzs,), (xs, zs), scratch, (turned,)
            )
        else:
            grad, dzs = run(backward_body, "layer_backward", meta, (grad,), near, (dzs,), (xs, zs), scratch)
            lead = grad
        if tick == ticks + 1:
            every = jnp.stack(
                [
                    jnp.where(depth == j, moved[0], jnp.where((depth - j) % LOW == 1, moved[1], moved[2]))
                    for j in range(LOW)
                ]
            )
            every, lead = lax.optimization_barrier((every, lead))
            every = lax.all_gather(every, ROW, axis=0, tiled=False)
        if tick < ticks + SECTIONS - 2:
            near = settle((own, other), lead)
        if tick < ticks - 1:
            block = lax.ppermute(block, "section", upward)
        if 0 <= behind and tick < ticks + SECTIONS - 2:
            grad = lax.ppermute(grad, "section", downward)
        if tick == ticks:
            moved.append(lax.ppermute(done, "zl", turns[2]))
        if tick == ticks - 1:
            done = acts[:micro]
            depth = lax.axis_index("zl")
            turns = [[(i, (i + k) % LOW) for i in range(LOW)] for k in range(LOW)]
            moved = [done, lax.ppermute(done, "zl", turns[1])]

    members = LOW * ACROSS * CORES
    piece = width // members
    theirs = lax.all_to_all(turned, ROW + ("zl",), 0, 0, tiled=True)
    partial = weight_partials(meta, theirs, every.reshape(members * micro * length, width))
    spread = lax.all_to_all(partial, SHARD, 0, 0, tiled=True)
    back = jnp.sum(spread.reshape(HIGH, members * OWN, 2 * piece).astype(jnp.float32), axis=0)
    back = back.reshape(LOW, ACROSS * CORES, OWN, 2, piece)
    owned = back.transpose(3, 2, 1, 0, 4).reshape(2, OWN, width)
    return owned[None]


def solution(mesh):
    fine = Mesh(mesh.devices.reshape(SECTIONS, HIGH, LOW, ACROSS, CORES), ("section",) + SHARD)
    placed = (
        P(None, SHARD, None, None),
        P(None, SHARD),
        P(),
        P("section"),
        P("section", None, SHARD, None),
        P(None, SHARD, None, None),
    )
    return jax.shard_map(
        shards, mesh=fine, in_specs=placed, out_specs=P("section", None, SHARD, None), check_vma=False
    )
```

```python
import jax
import jax.numpy as jnp
from jax import lax
from jax.experimental import pallas as pl
from jax.experimental.pallas import tpu as pltpu
from jax.sharding import Mesh, PartitionSpec as P

SECTIONS, HIGH, LOW, ACROSS, CORES = 8, 4, 3, 4, 2
OWN = 16
BLOCK = 256
CHUNKS = 4
LIMIT = 20 * 1024 * 1024
SHARD = ("zh", "zl", "x", "core")
DEEP = ("zh", "zl")
ROW = ("x", "core")
WIDE = ("zl", "x", "core")


def shifted(values, hours, limit_low):
    length = values.shape[0]
    row = lax.broadcasted_iota(jnp.int32, values.shape, 0)
    if limit_low:
        return jnp.where(row >= hours, pltpu.roll(values, hours, 0), 0.0)
    return jnp.where(row < length - hours, pltpu.roll(values, length - hours, 0), 0.0)


def norm_of(x_full):
    inverse = lax.rsqrt(jnp.mean(x_full * x_full, axis=-1, keepdims=True) + 1e-06)
    return inverse, x_full * inverse


def settle_body(*refs):
    count = (len(refs) - 2) // 2
    sems = refs[-1]
    copies = [
        pltpu.make_async_copy(refs[i], refs[count + 1 + i], sems.at[i]) for i in range(count)
    ]
    for copy in copies:
        copy.start()
    for copy in copies:
        copy.wait()


def settle(arrays, after):
    size = sum(v.size * v.dtype.itemsize for v in arrays)
    return pl.pallas_call(
        settle_body,
        out_shape=tuple(pltpu.VMEM(v.shape, v.dtype) for v in arrays),
        in_specs=[pl.BlockSpec(memory_space=pltpu.HBM)] * len(arrays) + [pl.BlockSpec(memory_space=pl.ANY)],
        out_specs=tuple(VMEM for _ in arrays),
        scratch_shapes=[pltpu.SemaphoreType.DMA((len(arrays),))],
        cost_estimate=pl.CostEstimate(flops=0, transcendentals=0, bytes_accessed=4 * size),
        compiler_params=pltpu.CompilerParams(vmem_limit_bytes=LIMIT),
        name="settle",
    )(*(pltpu.with_memory_space_constraint(v, pltpu.HBM) for v in arrays), after)


def ordered(meta, current, moved):
    even = meta[2] == 0
    first = jnp.where(even, current, moved).astype(jnp.bfloat16)
    second = jnp.where(even, moved, current).astype(jnp.bfloat16)
    return first, second


def forward_part(meta, x_ref, own_ref, other_ref, x_out, xs, zs, acts):
    slot = meta[0]
    x_full = x_ref[...].astype(jnp.float32)
    _, normed = norm_of(x_full)
    rounded = normed.astype(jnp.bfloat16)
    xs[slot] = x_ref[...]
    acts[slot] = rounded
    current = rounded.astype(jnp.float32)
    first, second = ordered(meta, current, shifted(current, meta[1], True))
    for start in range(0, x_ref.shape[1], BLOCK):
        cols = slice(start, start + BLOCK)
        pre = jnp.dot(first, own_ref[:, cols], preferred_element_type=jnp.float32)
        pre += jnp.dot(second, other_ref[:, cols], preferred_element_type=jnp.float32)
        zs[slot, :, cols] = pre
        x_out[:, cols] = (x_ref[:, cols].astype(jnp.float32) + pre * jax.nn.sigmoid(pre)).astype(jnp.bfloat16)


def backward_part(meta, g_ref, own_ref, other_ref, xs, zs, g_out, dzs, da):
    slot = meta[3]
    pre = zs[slot]
    sigma = jax.nn.sigmoid(pre)
    d_pre = g_ref[...].astype(jnp.float32) * sigma * (1.0 + pre * (1.0 - sigma))
    d_pre = d_pre.astype(jnp.bfloat16)
    dzs[slot] = d_pre
    current = d_pre.astype(jnp.float32)
    first, second = ordered(meta, current, shifted(current, meta[1], False))
    dims = (((1,), (1,)), ((), ()))
    for start in range(0, g_ref.shape[1], BLOCK):
        rows = slice(start, start + BLOCK)
        part = lax.dot_general(first, own_ref[rows, :], dims, preferred_element_type=jnp.float32)
        part += lax.dot_general(second, other_ref[rows, :], dims, preferred_element_type=jnp.float32)
        da[:, rows] = part
    inverse, normed = norm_of(xs[slot].astype(jnp.float32))
    d_norm = da[...]
    mean = jnp.mean(d_norm * normed, axis=-1, keepdims=True)
    g_out[...] = (g_ref[...].astype(jnp.float32) + inverse * (d_norm - normed * mean)).astype(jnp.bfloat16)


def forward_body(meta, x_ref, own_ref, other_ref, keep_x, keep_z, keep_a, x_out, xs, zs, acts):
    del keep_x, keep_z, keep_a
    forward_part(meta, x_ref, own_ref, other_ref, x_out, xs, zs, acts)


def backward_body(meta, g_ref, own_ref, other_ref, xs, zs, keep_d, g_out, dzs, da):
    del keep_d
    backward_part(meta, g_ref, own_ref, other_ref, xs, zs, g_out, dzs, da)


def last_body(meta, g_ref, xs, zs, keep_d, turned, dzs):
    del xs, keep_d
    slot = meta[3]
    pre = zs[slot]
    sigma = jax.nn.sigmoid(pre)
    d_pre = g_ref[...].astype(jnp.float32) * sigma * (1.0 + pre * (1.0 - sigma))
    dzs[slot] = d_pre.astype(jnp.bfloat16)
    hours_all = jnp.concatenate([dzs[i].astype(jnp.float32) for i in range(dzs.shape[0] - 1)], axis=0)
    turned[...] = hours_all.T.astype(jnp.bfloat16)


def weights_body(meta, turned, source_ref, out, every, sides, total, sems):
    depth = every.shape[0] // CHUNKS
    copies = []
    for index in range(CHUNKS):
        span = slice(index * depth, (index + 1) * depth)
        copies.append(pltpu.make_async_copy(source_ref.at[span], every.at[span], sems.at[index]))
        copies[-1].start()
    members = every.shape[0] // turned.shape[1]
    piece = turned.shape[0] // members
    length = turned.shape[1] // 2
    hours = meta[1]
    lane = lax.broadcasted_iota(jnp.int32, (piece, 2 * length), 1) % length
    for source in range(members):
        behind = meta[4] - source % LOW
        origin = source - source % LOW + jnp.where(behind < 0, behind + LOW, behind)
        current = turned[pl.ds(pl.multiple_of(origin * piece, piece), piece), :].astype(jnp.float32)
        moved = jnp.where(lane < length - hours, pltpu.roll(current, 2 * length - hours, 1), 0.0)
        lanes = slice(source * 2 * length, (source + 1) * 2 * length)
        sides[:piece, lanes] = current.astype(jnp.bfloat16)
        sides[piece:, lanes] = moved.astype(jnp.bfloat16)
    for index in range(CHUNKS):
        copies[index].wait()
        span = slice(index * depth, (index + 1) * depth)
        for start in range(0, every.shape[1], BLOCK):
            cols = slice(start, start + BLOCK)
            part = jnp.dot(sides[:, span], every[span, cols], preferred_element_type=jnp.float32)
            if index > 0:
                part += total[:, cols]
            if index < CHUNKS - 1:
                total[:, cols] = part
                continue
            out[cols, :] = part.T.astype(jnp.bfloat16)


def weight_partials(meta, turned, every):
    tokens, width = every.shape
    piece = width * turned.shape[1] // tokens
    return pl.pallas_call(
        weights_body,
        out_shape=jax.ShapeDtypeStruct((width, 2 * piece), jnp.bfloat16),
        in_specs=[SMEM, VMEM, pl.BlockSpec(memory_space=pltpu.HBM)],
        out_specs=VMEM,
        scratch_shapes=[
            pltpu.VMEM(every.shape, every.dtype),
            pltpu.VMEM((2 * piece, tokens), jnp.bfloat16),
            pltpu.VMEM((2 * piece, width), jnp.float32),
            pltpu.SemaphoreType.DMA((CHUNKS,)),
        ],
        compiler_params=pltpu.CompilerParams(vmem_limit_bytes=LIMIT),
        name="weight_partials",
    )(meta, turned, pltpu.with_memory_space_constraint(every, pltpu.HBM))


def turn_body(
    meta, x_ref, g_ref, own_ref, other_ref, keep_x, keep_z, keep_a, keep_d, x_out, g_out, xs, zs, acts, dzs, da
):
    del keep_x, keep_z, keep_a, keep_d
    forward_part(meta, x_ref, own_ref, other_ref, x_out, xs, zs, acts)
    backward_part(meta, g_ref, own_ref, other_ref, xs, zs, g_out, dzs, da)


VMEM = pl.BlockSpec(memory_space=pltpu.VMEM)
SMEM = pl.BlockSpec(memory_space=pltpu.SMEM)


def run(body, name, meta, free, weights, kept, read, scratch, extra=()):
    operands = (meta, *free, *weights, *read, *kept)
    first = len(operands) - len(kept)
    return pl.pallas_call(
        body,
        out_shape=tuple(jax.ShapeDtypeStruct(v.shape, v.dtype) for v in (*free, *extra))
        + tuple(pltpu.VMEM(v.shape, v.dtype) for v in kept),
        in_specs=[SMEM] + [VMEM] * (len(operands) - 1),
        out_specs=tuple(VMEM for _ in range(len(free) + len(extra) + len(kept))),
        scratch_shapes=scratch,
        input_output_aliases={first + i: len(free) + len(extra) + i for i in range(len(kept))},
        compiler_params=pltpu.CompilerParams(vmem_limit_bytes=LIMIT),
        name=name,
    )(*operands)


def shards(features, index, table, exponent, weights, cotangent):
    here = lax.axis_index("section")
    micro, _, length, width = features.shape
    hours = jnp.left_shift(jnp.int32(1), exponent[0])
    onehot = (index[:, :, None] == jnp.arange(table.shape[0], dtype=jnp.int32)).astype(jnp.bfloat16)
    bias = jnp.einsum("mwb,bc->mwc", onehot, table, preferred_element_type=jnp.float32)
    inputs = (features.astype(jnp.float32) + bias[:, :, None, :]).astype(jnp.bfloat16)[:, 0]
    upstream = cotangent[:, 0]
    core = lax.axis_index("core")
    depth = lax.axis_index("zl")
    tap = weights[0]
    copies = jnp.broadcast_to(tap[None], (ACROSS,) + tap.shape).reshape(ACROSS * CORES * OWN, width)
    row = lax.all_to_all(copies, ROW, 0, 0, tiled=True)
    own = lax.all_gather(row, DEEP, axis=0, tiled=True)
    other = lax.ppermute(own, "core", [(0, 1), (1, 0)])

    ticks = SECTIONS + micro - 1
    slots = (micro + 1, length, width)
    xs = jnp.zeros(slots, jnp.bfloat16)
    acts = jnp.zeros(slots, jnp.bfloat16)
    zs = jnp.zeros(slots, jnp.float32)
    dzs = jnp.zeros(slots, jnp.bfloat16)
    scratch = [pltpu.VMEM((length, width), jnp.float32)]

    def slot_of(order):
        return jnp.where(jnp.logical_and(order >= 0, order < micro), order, micro)

    def meta_of(ahead, behind):
        parts = [slot_of(ahead - here), hours, core, slot_of(behind - (SECTIONS - 1 - here)), depth]
        return jnp.stack(parts).astype(jnp.int32)

    upward = [(i, i + 1) for i in range(SECTIONS - 1)]
    downward = [(i + 1, i) for i in range(SECTIONS - 1)]

    block = inputs[0]
    grad = upstream[0]
    near = settle((own,), inputs) + settle((other,), inputs)
    for tick in range(ticks + SECTIONS - 1):
        behind = tick - (SECTIONS - 1)
        meta = meta_of(tick, behind)
        if 0 < tick < micro:
            block = jnp.where(here == 0, inputs[tick], block)
        if 0 < behind < micro:
            grad = jnp.where(here == SECTIONS - 1, upstream[behind], grad)
        if behind < 0:
            block, xs, zs, acts = run(forward_body, "layer_forward", meta, (block,), near, (xs, zs, acts), (), [])
            lead = block
        elif tick < ticks:
            block, grad, xs, zs, acts, dzs = run(
                turn_body, "layer_turn", meta, (block, grad), near, (xs, zs, acts, dzs), (), scratch
            )
            lead = grad
        elif tick == ticks + SECTIONS - 2:
            turned = jax.ShapeDtypeStruct((width, micro * length), jnp.bfloat16)
            turned, dzs = run(last_body, "layer_last", meta, (), (), (dzs,), (grad, xs, zs), [], (turned,))
        else:
            grad, dzs = run(backward_body, "layer_backward", meta, (grad,), near, (dzs,), (xs, zs), scratch)
            lead = grad
        if tick == ticks + 1:
            every = jnp.stack(moved)
            every, lead = lax.optimization_barrier((every, lead))
            every = lax.all_gather(every, ROW, axis=0, tiled=False)
        if tick < ticks + SECTIONS - 3:
            near = settle((own, other), lead)
        if tick < ticks - 1:
            block = lax.ppermute(block, "section", upward)
        if 0 <= behind and tick < ticks + SECTIONS - 2:
            grad = lax.ppermute(grad, "section", downward)
        if tick == ticks:
            moved.append(lax.ppermute(done, "zl", turns[2]))
        if tick == ticks - 1:
            done = acts[:micro]
            turns = [[(i, (i + k) % LOW) for i in range(LOW)] for k in range(LOW)]
            moved = [done, lax.ppermute(done, "zl", turns[1])]

    members = LOW * ACROSS * CORES
    piece = width // members
    theirs = lax.all_to_all(turned, ROW + ("zl",), 0, 0, tiled=True)
    partial = weight_partials(meta, theirs, every.reshape(members * micro * length, width))
    spread = lax.all_to_all(partial, SHARD, 0, 0, tiled=True)
    back = jnp.sum(spread.reshape(HIGH, members * OWN, 2 * piece).astype(jnp.float32), axis=0)
    back = back.reshape(LOW, ACROSS * CORES, OWN, 2, piece)
    owned = back.transpose(3, 2, 1, 0, 4).reshape(2, OWN, width)
    return owned[None]


def solution(mesh):
    fine = Mesh(mesh.devices.reshape(SECTIONS, HIGH, LOW, ACROSS, CORES), ("section",) + SHARD)
    placed = (
        P(None, SHARD, None, None),
        P(None, SHARD),
        P(),
        P("section"),
        P("section", None, SHARD, None),
        P(None, SHARD, None, None),
    )
    return jax.shard_map(
        shards, mesh=fine, in_specs=placed, out_specs=P("section", None, SHARD, None), check_vma=False
    )
```

```python
import jax
import jax.numpy as jnp
from jax import lax
from jax.experimental import pallas as pl
from jax.experimental.pallas import tpu as pltpu
from jax.sharding import Mesh, PartitionSpec as P

SECTIONS, HIGH, LOW, ACROSS, CORES = 8, 4, 3, 4, 2
OWN = 16
BLOCK = 256
CHUNKS = 4
LIMIT = 20 * 1024 * 1024
SHARD = ("zh", "zl", "x", "core")
DEEP = ("zh", "zl")
ROW = ("x", "core")
WIDE = ("zl", "x", "core")


def shifted(values, hours, limit_low):
    length = values.shape[0]
    row = lax.broadcasted_iota(jnp.int32, values.shape, 0)
    if limit_low:
        return jnp.where(row >= hours, pltpu.roll(values, hours, 0), 0.0)
    return jnp.where(row < length - hours, pltpu.roll(values, length - hours, 0), 0.0)


def norm_of(x_full):
    inverse = lax.rsqrt(jnp.mean(x_full * x_full, axis=-1, keepdims=True) + 1e-06)
    return inverse, x_full * inverse


def settle_body(*refs):
    count = (len(refs) - 2) // 2
    sems = refs[-1]
    copies = [
        pltpu.make_async_copy(refs[i], refs[count + 1 + i], sems.at[i]) for i in range(count)
    ]
    for copy in copies:
        copy.start()
    for copy in copies:
        copy.wait()


def settle(arrays, after):
    size = sum(v.size * v.dtype.itemsize for v in arrays)
    return pl.pallas_call(
        settle_body,
        out_shape=tuple(pltpu.VMEM(v.shape, v.dtype) for v in arrays),
        in_specs=[pl.BlockSpec(memory_space=pltpu.HBM)] * len(arrays) + [pl.BlockSpec(memory_space=pl.ANY)],
        out_specs=tuple(VMEM for _ in arrays),
        scratch_shapes=[pltpu.SemaphoreType.DMA((len(arrays),))],
        cost_estimate=pl.CostEstimate(flops=0, transcendentals=0, bytes_accessed=4 * size),
        compiler_params=pltpu.CompilerParams(vmem_limit_bytes=LIMIT),
        name="settle",
    )(*(pltpu.with_memory_space_constraint(v, pltpu.HBM) for v in arrays), after)


def ordered(meta, current, moved):
    even = meta[2] == 0
    first = jnp.where(even, current, moved).astype(jnp.bfloat16)
    second = jnp.where(even, moved, current).astype(jnp.bfloat16)
    return first, second


def forward_part(meta, x_ref, own_ref, other_ref, x_out, xs, zs, acts):
    slot = meta[0]
    x_full = x_ref[...].astype(jnp.float32)
    _, normed = norm_of(x_full)
    rounded = normed.astype(jnp.bfloat16)
    xs[slot] = x_ref[...]
    acts[slot] = rounded
    current = rounded.astype(jnp.float32)
    first, second = ordered(meta, current, shifted(current, meta[1], True))
    for start in range(0, x_ref.shape[1], BLOCK):
        cols = slice(start, start + BLOCK)
        pre = jnp.dot(first, own_ref[:, cols], preferred_element_type=jnp.float32)
        pre += jnp.dot(second, other_ref[:, cols], preferred_element_type=jnp.float32)
        zs[slot, :, cols] = pre
        x_out[:, cols] = (x_ref[:, cols].astype(jnp.float32) + pre * jax.nn.sigmoid(pre)).astype(jnp.bfloat16)


def backward_part(meta, g_ref, own_ref, other_ref, xs, zs, g_out, dzs, da):
    slot = meta[3]
    pre = zs[slot]
    sigma = jax.nn.sigmoid(pre)
    d_pre = g_ref[...].astype(jnp.float32) * sigma * (1.0 + pre * (1.0 - sigma))
    d_pre = d_pre.astype(jnp.bfloat16)
    dzs[slot] = d_pre
    current = d_pre.astype(jnp.float32)
    first, second = ordered(meta, current, shifted(current, meta[1], False))
    dims = (((1,), (1,)), ((), ()))
    for start in range(0, g_ref.shape[1], BLOCK):
        rows = slice(start, start + BLOCK)
        part = lax.dot_general(first, own_ref[rows, :], dims, preferred_element_type=jnp.float32)
        part += lax.dot_general(second, other_ref[rows, :], dims, preferred_element_type=jnp.float32)
        da[:, rows] = part
    inverse, normed = norm_of(xs[slot].astype(jnp.float32))
    d_norm = da[...]
    mean = jnp.mean(d_norm * normed, axis=-1, keepdims=True)
    g_out[...] = (g_ref[...].astype(jnp.float32) + inverse * (d_norm - normed * mean)).astype(jnp.bfloat16)


def forward_body(meta, x_ref, own_ref, other_ref, keep_x, keep_z, keep_a, x_out, xs, zs, acts):
    del keep_x, keep_z, keep_a
    forward_part(meta, x_ref, own_ref, other_ref, x_out, xs, zs, acts)


def backward_body(meta, g_ref, own_ref, other_ref, xs, zs, keep_d, g_out, dzs, da):
    del keep_d
    backward_part(meta, g_ref, own_ref, other_ref, xs, zs, g_out, dzs, da)


def last_body(meta, g_ref, xs, zs, keep_d, turned, dzs):
    del xs, keep_d
    slot = meta[3]
    pre = zs[slot]
    sigma = jax.nn.sigmoid(pre)
    d_pre = g_ref[...].astype(jnp.float32) * sigma * (1.0 + pre * (1.0 - sigma))
    dzs[slot] = d_pre.astype(jnp.bfloat16)
    hours_all = jnp.concatenate([dzs[i].astype(jnp.float32) for i in range(dzs.shape[0] - 1)], axis=0)
    turned[...] = hours_all.T.astype(jnp.bfloat16)


def weights_body(meta, turned, source_ref, out, every, sides, total, sems):
    depth = every.shape[0] // CHUNKS
    copies = []
    for index in range(CHUNKS):
        span = slice(index * depth, (index + 1) * depth)
        copies.append(pltpu.make_async_copy(source_ref.at[span], every.at[span], sems.at[index]))
        copies[-1].start()
    members = every.shape[0] // turned.shape[1]
    piece = turned.shape[0] // members
    length = turned.shape[1] // 2
    hours = meta[1]
    lane = lax.broadcasted_iota(jnp.int32, (piece, 2 * length), 1) % length
    for source in range(members):
        behind = meta[4] - source % LOW
        origin = source - source % LOW + jnp.where(behind < 0, behind + LOW, behind)
        current = turned[pl.ds(pl.multiple_of(origin * piece, piece), piece), :].astype(jnp.float32)
        moved = jnp.where(lane < length - hours, pltpu.roll(current, 2 * length - hours, 1), 0.0)
        lanes = slice(source * 2 * length, (source + 1) * 2 * length)
        sides[:piece, lanes] = current.astype(jnp.bfloat16)
        sides[piece:, lanes] = moved.astype(jnp.bfloat16)
    for index in range(CHUNKS):
        copies[index].wait()
        span = slice(index * depth, (index + 1) * depth)
        for start in range(0, every.shape[1], BLOCK):
            cols = slice(start, start + BLOCK)
            part = jnp.dot(sides[:, span], every[span, cols], preferred_element_type=jnp.float32)
            if index > 0:
                part += total[:, cols]
            if index < CHUNKS - 1:
                total[:, cols] = part
                continue
            out[cols, :] = part.T.astype(jnp.bfloat16)


def weight_partials(meta, turned, every):
    tokens, width = every.shape
    piece = width * turned.shape[1] // tokens
    return pl.pallas_call(
        weights_body,
        out_shape=jax.ShapeDtypeStruct((width, 2 * piece), jnp.bfloat16),
        in_specs=[SMEM, VMEM, pl.BlockSpec(memory_space=pltpu.HBM)],
        out_specs=VMEM,
        scratch_shapes=[
            pltpu.VMEM(every.shape, every.dtype),
            pltpu.VMEM((2 * piece, tokens), jnp.bfloat16),
            pltpu.VMEM((2 * piece, width), jnp.float32),
            pltpu.SemaphoreType.DMA((CHUNKS,)),
        ],
        compiler_params=pltpu.CompilerParams(vmem_limit_bytes=LIMIT),
        name="weight_partials",
    )(meta, turned, pltpu.with_memory_space_constraint(every, pltpu.HBM))


def turn_body(
    meta, x_ref, g_ref, own_ref, other_ref, keep_x, keep_z, keep_a, keep_d, x_out, g_out, xs, zs, acts, dzs, da
):
    del keep_x, keep_z, keep_a, keep_d
    forward_part(meta, x_ref, own_ref, other_ref, x_out, xs, zs, acts)
    backward_part(meta, g_ref, own_ref, other_ref, xs, zs, g_out, dzs, da)


VMEM = pl.BlockSpec(memory_space=pltpu.VMEM)
SMEM = pl.BlockSpec(memory_space=pltpu.SMEM)


def run(body, name, meta, free, weights, kept, read, scratch, extra=()):
    operands = (meta, *free, *weights, *read, *kept)
    first = len(operands) - len(kept)
    return pl.pallas_call(
        body,
        out_shape=tuple(jax.ShapeDtypeStruct(v.shape, v.dtype) for v in (*free, *extra))
        + tuple(pltpu.VMEM(v.shape, v.dtype) for v in kept),
        in_specs=[SMEM] + [VMEM] * (len(operands) - 1),
        out_specs=tuple(VMEM for _ in range(len(free) + len(extra) + len(kept))),
        scratch_shapes=scratch,
        input_output_aliases={first + i: len(free) + len(extra) + i for i in range(len(kept))},
        compiler_params=pltpu.CompilerParams(vmem_limit_bytes=LIMIT),
        name=name,
    )(*operands)


def shards(features, index, table, exponent, weights, cotangent):
    here = lax.axis_index("section")
    micro, _, length, width = features.shape
    hours = jnp.left_shift(jnp.int32(1), exponent[0])
    onehot = (index[:, :, None] == jnp.arange(table.shape[0], dtype=jnp.int32)).astype(jnp.bfloat16)
    bias = jnp.einsum("mwb,bc->mwc", onehot, table, preferred_element_type=jnp.float32)
    inputs = (features.astype(jnp.float32) + bias[:, :, None, :]).astype(jnp.bfloat16)[:, 0]
    upstream = cotangent[:, 0]
    core = lax.axis_index("core")
    depth = lax.axis_index("zl")
    tap = weights[0]
    copies = jnp.broadcast_to(tap[None], (ACROSS,) + tap.shape).reshape(ACROSS * CORES * OWN, width)
    row = lax.all_to_all(copies, ROW, 0, 0, tiled=True)
    own = lax.all_gather(row, DEEP, axis=0, tiled=True)
    other = lax.ppermute(own, "core", [(0, 1), (1, 0)])

    ticks = SECTIONS + micro - 1
    slots = (micro + 1, length, width)
    xs = jnp.zeros(slots, jnp.bfloat16)
    acts = jnp.zeros(slots, jnp.bfloat16)
    zs = jnp.zeros(slots, jnp.float32)
    dzs = jnp.zeros(slots, jnp.bfloat16)
    scratch = [pltpu.VMEM((length, width), jnp.float32)]

    def slot_of(order):
        return jnp.where(jnp.logical_and(order >= 0, order < micro), order, micro)

    def meta_of(ahead, behind):
        parts = [slot_of(ahead - here), hours, core, slot_of(behind - (SECTIONS - 1 - here)), depth]
        return jnp.stack(parts).astype(jnp.int32)

    upward = [(i, i + 1) for i in range(SECTIONS - 1)]
    downward = [(i + 1, i) for i in range(SECTIONS - 1)]

    block = inputs[0]
    grad = upstream[0]
    near = settle((own,), inputs) + settle((other,), inputs)
    for tick in range(ticks + SECTIONS - 1):
        behind = tick - (SECTIONS - 1)
        meta = meta_of(tick, behind)
        if 0 < tick < micro:
            block = jnp.where(here == 0, inputs[tick], block)
        if 0 < behind < micro:
            grad = jnp.where(here == SECTIONS - 1, upstream[behind], grad)
        if behind < 0:
            block, xs, zs, acts = run(forward_body, "layer_forward", meta, (block,), near, (xs, zs, acts), (), [])
            lead = block
        elif tick < ticks:
            block, grad, xs, zs, acts, dzs = run(
                turn_body, "layer_turn", meta, (block, grad), near, (xs, zs, acts, dzs), (), scratch
            )
            lead = grad
        elif tick == ticks + SECTIONS - 2:
            turned = jax.ShapeDtypeStruct((width, micro * length), jnp.bfloat16)
            turned, dzs = run(last_body, "layer_last", meta, (), (), (dzs,), (grad, xs, zs), [], (turned,))
        else:
            grad, dzs = run(backward_body, "layer_backward", meta, (grad,), near, (dzs,), (xs, zs), scratch)
            lead = grad
        if tick == ticks + 1:
            every = jnp.stack(moved)
            every, lead = lax.optimization_barrier((every, lead))
            every = lax.all_gather(every, ROW, axis=0, tiled=False)
        if tick < ticks + SECTIONS - 3:
            near = settle((own, other), lead)
        if tick < ticks - 1:
            block = lax.ppermute(block, "section", upward)
        if 0 <= behind and tick < ticks + SECTIONS - 2:
            grad = lax.ppermute(grad, "section", downward)
        if tick == ticks:
            done, _ = lax.optimization_barrier((done, lead))
            moved.append(lax.ppermute(done, "zl", turns[2]))
        if tick == ticks - 1:
            done = acts[:micro]
            turns = [[(i, (i + k) % LOW) for i in range(LOW)] for k in range(LOW)]
            moved = [done, lax.ppermute(done, "zl", turns[1])]

    members = LOW * ACROSS * CORES
    piece = width // members
    theirs = lax.all_to_all(turned, ROW + ("zl",), 0, 0, tiled=True)
    partial = weight_partials(meta, theirs, every.reshape(members * micro * length, width))
    spread = lax.all_to_all(partial, SHARD, 0, 0, tiled=True)
    back = jnp.sum(spread.reshape(HIGH, members * OWN, 2 * piece).astype(jnp.float32), axis=0)
    back = back.reshape(LOW, ACROSS * CORES, OWN, 2, piece)
    owned = back.transpose(3, 2, 1, 0, 4).reshape(2, OWN, width)
    return owned[None]


def solution(mesh):
    fine = Mesh(mesh.devices.reshape(SECTIONS, HIGH, LOW, ACROSS, CORES), ("section",) + SHARD)
    placed = (
        P(None, SHARD, None, None),
        P(None, SHARD),
        P(),
        P("section"),
        P("section", None, SHARD, None),
        P(None, SHARD, None, None),
    )
    return jax.shard_map(
        shards, mesh=fine, in_specs=placed, out_specs=P("section", None, SHARD, None), check_vma=False
    )
```
